128 devices in a mesh: replica: 32 (over y, x, z_lo), tensor: 4 (over z_hi, core).
Axes of the slice: x: 4, y: 4, z: 4 (z_hi: 2, z_lo: 2; z = z_hi * 2 + z_lo), core: 2. Of those that a mesh axis runs over, the one named last changes fastest.
Arguments:
- weight: bfloat16 [32, 4096, 2048], P('replica', None, 'tensor'), may hold values from -0.09375 to 0.09375
- momentum: bfloat16 [32, 4096, 2048], P('replica', None, 'tensor'), may hold values from -24 to 24
- inputs: bfloat16 [2, 16384, 4096], P(None, ('replica', 'tensor')), may hold values from -6 to 6
- out_grads: bfloat16 [2, 16384, 2048], P(None, 'replica', 'tensor'), may hold values from -6 to 6
Outputs:
- new_weight: bfloat16 [32, 4096, 2048], P('replica', None, 'tensor')
- new_momentum: bfloat16 [32, 4096, 2048], P('replica', None, 'tensor')
- input_grad: bfloat16 [2, 16384, 4096], P(None, ('replica', 'tensor'))
The draws below stay inside these ranges and needn't reach their ends.
All inputs are finite; a program needn't handle non-finite values.
Results may differ from the reference program's by a relative error of at most 0.014.
Values may be sent and summed in bfloat16 or wider, within the bound.
A program may use at most 128 MiB of HBM per device.

```python
import jax
import jax.numpy as jnp
from jax import lax

D = 4096
DOUT = 2048
ROWS = 512
STEPS = 2
REPLICAS = 32
TOTAL_ROWS = 16384
N_TENSOR = 4


def levels(stream_key, dims, split, least, top_value):
    level = 1.0
    for position, blocks in split:
        heights = jax.random.uniform(jax.random.fold_in(jax.random.fold_in(stream_key, 6), position), (blocks,), jnp.float32, least / len(split), top_value / len(split))
        level = level * jnp.repeat(jnp.exp(heights), dims[position] // blocks).reshape((-1,) + (1,) * (len(dims) - 1 - position))
    return level


def gaussian(rng, extent, scale, most, shards=(), kind=jnp.bfloat16):
    result = jax.random.normal(rng, extent, jnp.float32) * scale
    if len(shards) > 0:
        result = levels(rng, extent, shards, -0.22, 0.18) * result
    return jnp.clip(result, min=-most, max=most).astype(kind)


def setup_inputs(seed: int = 0) -> dict:
    seeds = jax.random.split(jax.random.key(seed), 5)
    return {
        "weight": gaussian(seeds[0], (REPLICAS, D, DOUT), D ** -0.5, 0.09375, ((0, 32), (2, 4))),
        "momentum": gaussian(seeds[1], (REPLICAS, D, DOUT), 4.0, 24.0, ((0, 32), (2, 4))),
        "inputs": gaussian(seeds[2], (STEPS, TOTAL_ROWS, D), 1.0, 6.0, ((1, 128),)),
        "out_grads": gaussian(seeds[3], (STEPS, TOTAL_ROWS, DOUT), 1.0, 6.0, ((1, 32), (2, 4))),
    }


learn_rate = 0.001
mom_decay = 0.9


def silu_slope(pre):
    sigma = jax.nn.sigmoid(pre)
    return sigma * (1.0 + pre * (1.0 - sigma))


def reference(weight, momentum, inputs, out_grads):
    replicas = weight.shape[0]
    indices = jnp.arange(replicas, dtype=jnp.int32)
    blocks = DOUT // N_TENSOR
    weight_now = weight
    moment_now = momentum
    grads_out = []
    for step in range(STEPS):
        rows_in = inputs[step].reshape(replicas, ROWS, D).astype(jnp.float32)
        pre = jnp.einsum('rnd,rdk->rnk', rows_in, weight_now.astype(jnp.float32))
        upstream = out_grads[step].reshape(replicas, ROWS, DOUT).astype(jnp.float32)
        slope_grad = (upstream * silu_slope(pre)).astype(jnp.bfloat16)
        grad_w = jnp.einsum('rnd,rnk->rdk', rows_in, slope_grad.astype(jnp.float32))
        partial_value = jnp.einsum('rntc,rdtc->rtnd',
                             slope_grad.reshape(replicas, ROWS, N_TENSOR, blocks).astype(jnp.float32),
                             weight_now.reshape(replicas, D, N_TENSOR, blocks).astype(jnp.float32))
        partial_value = lax.optimization_barrier(partial_value.astype(jnp.bfloat16)).astype(jnp.float32)
        grads_out.append(jnp.sum(partial_value, axis=1).astype(jnp.bfloat16).reshape(replicas * ROWS, D))
        moment_new = (mom_decay * moment_now.astype(jnp.float32) + grad_w).astype(jnp.bfloat16)
        stepped = (weight_now.astype(jnp.float32) - learn_rate * moment_new.astype(jnp.float32)).astype(jnp.bfloat16)
        partner = jnp.bitwise_xor(indices, jnp.int32(1 << step))
        weight_now = ((stepped.astype(jnp.float32) + stepped[partner].astype(jnp.float32)) * 0.5).astype(jnp.bfloat16)
        moment_now = ((moment_new.astype(jnp.float32) + moment_new[partner].astype(jnp.float32)) * 0.5).astype(jnp.bfloat16)
    return weight_now, moment_now, jnp.stack(grads_out)
```

```python
import jax
import jax.numpy as jnp
from jax import lax
from jax.sharding import PartitionSpec as P

learn_rate = 0.001
mom_decay = 0.9

AXES = ("replica", "tensor")
CORE = 1
NEAR = 4
FAR = 6
ACROSS = 8

bf16 = jnp.bfloat16
f32 = jnp.float32


def hop(block, mask):
    count = lax.axis_size("replica") * lax.axis_size("tensor")
    return lax.ppermute(block, AXES, [(i, i ^ mask) for i in range(count)])


def silu_slope(pre):
    sigma = jax.nn.sigmoid(pre)
    return sigma * (1.0 + pre * (1.0 - sigma))


def cat(*parts):
    return jnp.concatenate(parts, axis=0)


def dot(a, b, dims):
    return lax.dot_general(a, b, (dims, ((), ())), preferred_element_type=f32)


def gossip_mean(own, lower):
    half = own.shape[0] // 2
    keep = lax.dynamic_slice_in_dim(own, lower * half, half, 0)
    give = lax.dynamic_slice_in_dim(own, (1 - lower) * half, half, 0)
    got = hop(give, ACROSS)
    pair = ((keep.astype(f32) + got.astype(f32)) * 0.5).astype(bf16)
    other = hop(pair, NEAR)
    mean = ((pair.astype(f32) + other.astype(f32)) * 0.5).astype(bf16)
    rest = hop(mean, ACROSS)
    full = lax.dynamic_update_slice_in_dim(jnp.zeros_like(own), mean, lower * half, 0)
    return lax.dynamic_update_slice_in_dim(full, rest, (1 - lower) * half, 0)


def local(weight, momentum, inputs, out_grads):
    w = weight[0]
    m = momentum[0]
    r = lax.axis_index("replica")
    t = lax.axis_index("tensor")
    lower = (r // 2) % 2
    rows = inputs.shape[1]
    cut = rows // 2
    x0 = inputs[0]
    x1 = inputs[1]

    def in_order(grads):
        blocks = [lax.dynamic_slice_in_dim(grads, (t ^ j) * rows, rows, 0) for j in (0, 2, 1, 3)]
        return cat(*blocks)

    via_far = hop(x0[:cut], FAR)
    via_near = hop(x0[cut:], NEAR)
    x0_pair = cat(x0, hop(via_far, NEAR), hop(via_near, FAR))
    x_first = cat(x0_pair, hop(x0_pair, CORE))

    b_near = hop(x1, NEAR)
    b_far = hop(x1, FAR)
    a_pair = cat(x1, hop(b_far[:cut], NEAR), hop(b_near[cut:], FAR))
    ab = cat(a_pair, b_near, b_far)
    ab_other = hop(ab, CORE)
    x_a = cat(a_pair, ab_other[: 2 * rows])
    x_ab = cat(x_a, ab[2 * rows :], ab_other[2 * rows :])
    c_pair = hop(a_pair, ACROSS)
    x_c = cat(c_pair, hop(c_pair, CORE))

    w_mean = gossip_mean(w, lower)

    pre = dot(x_first, w, ((1,), (0,)))
    slope0 = (in_order(out_grads[0]).astype(f32) * silu_slope(pre)).astype(bf16)
    grad_w = dot(x_first, slope0, ((0,), (0,)))
    moment = (mom_decay * m.astype(f32) + grad_w).astype(bf16)
    stepped = (w.astype(f32) - learn_rate * moment.astype(f32)).astype(bf16)
    m_mean = gossip_mean(moment, lower)

    both = dot(x_ab, stepped, ((1,), (0,)))
    n = 4 * rows
    pre1 = (both[:n] + hop(both[n:], NEAR)) * 0.5
    slope1 = (in_order(out_grads[1]).astype(f32) * silu_slope(pre1)).astype(bf16)
    slope1_b = hop(slope1, NEAR)
    slope1_c = hop(slope1, ACROSS)

    part0 = dot(slope0, w, ((1,), (1,))).astype(bf16)
    chip0 = part0[: 2 * rows].astype(f32) + hop(part0[2 * rows :], CORE).astype(f32)
    away0 = chip0[rows:].astype(bf16)
    back = cat(hop(hop(away0[:cut], FAR), NEAR), hop(hop(away0[cut:], NEAR), FAR))
    grad_in0 = (chip0[:rows] + back.astype(f32)).astype(bf16)

    part1 = (dot(cat(slope1, slope1_b), stepped, ((1,), (1,))) * 0.5).astype(bf16)
    got1 = hop(cat(part1[2 * rows : n], part1[n + 2 * rows :]), CORE).astype(f32)
    chip_a = part1[: 2 * rows].astype(f32) + got1[: 2 * rows]
    chip_b = part1[n : n + 2 * rows].astype(f32) + got1[2 * rows :]
    away1 = chip_a[rows:].astype(bf16)
    for_far = hop(away1[:cut], NEAR).astype(f32)
    for_near = hop(away1[cut:], FAR).astype(f32)
    to_near = cat(chip_b[:cut], chip_b[cut:rows] + for_near).astype(bf16)
    to_far = cat(chip_b[rows : rows + cut] + for_far, chip_b[rows + cut :]).astype(bf16)
    grad_in1 = (
        chip_a[:rows] + hop(to_near, NEAR).astype(f32) + hop(to_far, FAR).astype(f32)
    ).astype(bf16)

    grad1 = dot(cat(x_a, x_c), cat(slope1, slope1_c), ((0,), (0,))) * 0.5
    m_mean = m_mean.astype(f32)
    new_m = (mom_decay * m_mean + grad1).astype(bf16)
    new_w = (w_mean.astype(f32) - learn_rate * (m_mean + new_m.astype(f32))).astype(bf16)
    return (new_w[None], new_m[None], jnp.stack([grad_in0, grad_in1]))


def solution(mesh):
    return jax.shard_map(
        local,
        mesh=mesh,
        in_specs=(
            P("replica", None, "tensor"),
            P("replica", None, "tensor"),
            P(None, ("replica", "tensor"), None),
            P(None, "replica", "tensor"),
        ),
        out_specs=(
            P("replica", None, "tensor"),
            P("replica", None, "tensor"),
            P(None, ("replica", "tensor"), None),
        ),
        check_vma=False,
    )
```

```python
import jax
import jax.numpy as jnp
from jax import lax
from jax.experimental import pallas as pl
from jax.experimental.pallas import tpu as pltpu
from jax.sharding import PartitionSpec as P

learn_rate = 0.001
mom_decay = 0.9

bf16 = jnp.bfloat16
f32 = jnp.float32

CHUNKS = 4
TRANSFERS = (
    "x0n", "x0f", "x0c0", "x0fn", "x0nf", "x0c1", "x1n", "x1f", "x1c", "x1fn", "x1nf", "x1c1",
    "xbc", "xca", "xcb", "xcc", "q", "s1n", "s1x", "s1c", "s1bc", "st", "p0c", "a0f", "a0n", "a0fn",
    "a0nf", "a1n", "a1f", "to_near", "to_far",
)
NUMBER = {name: k for k, name in enumerate(TRANSFERS)}
CHAINS = {name: len(TRANSFERS) + CHUNKS * k for k, name in enumerate(("w1", "w2", "w3", "m1", "m2", "m3"))}
COPIES = len(TRANSFERS) + CHUNKS * len(CHAINS)


def silu_slope(pre):
    sigma = jax.nn.sigmoid(pre)
    return sigma * (1.0 + pre * (1.0 - sigma))


def dot(a, b, left, right):
    return lax.dot_general(a, b, (((left,), (right,)), ((), ())), preferred_element_type=f32)


def kernel(
    w_hbm, m_hbm, x_hbm, og_hbm, new_w, new_m, grad_in,
    wv, mv, stepped, stepped_o, x0, xa, xb, xc, lw1, lw2, lw3, lm1, lm2, lm3,
    tn, tf, lp0, t0n, t0f, r0n, r0f, t1n, t1f, r1n, r1f,
    q_own, q_give, q_got, og, s0, s1, s1b, s1c, s1o, s1bo,
    send, recv, local,
):
    d, cols = wv.shape
    rows = x0.shape[0] // 4
    cut = rows // 2
    half = d // 2
    chunk = half // CHUNKS
    tile = chunk // 2
    pair = 2 * rows
    n = 4 * rows

    r = lax.axis_index("replica")
    t = lax.axis_index("tensor")
    lower = (r // 2) % 2
    keep0 = lower * half
    give0 = (1 - lower) * half
    r_near = r + 1 - 2 * (r % 2)
    t_core = t + 1 - 2 * (t % 2)
    t_far = (t + 2) % 4
    core = (r, t_core)
    near = (r_near, t)
    far = (r_near, t_far)
    across = (r + 2 - 4 * lower, t)

    barrier = pltpu.get_barrier_semaphore()
    for there in (core, near, far, across):
        pl.semaphore_signal(barrier, inc=1, device_id=there, device_id_type=pl.DeviceIdType.MESH)
    pl.semaphore_wait(barrier, 4)

    def piece(start, size):
        return pl.ds(pl.multiple_of(start, size), size)

    def remote(k, src, dst, there):
        return pltpu.make_async_remote_copy(
            src_ref=src, dst_ref=dst, send_sem=send.at[k], recv_sem=recv.at[k],
            device_id=there, device_id_type=pl.DeviceIdType.MESH,
        )

    routes = {
        "x0n": (x_hbm.at[0, pl.ds(cut, cut)], tn, near),
        "x0f": (x_hbm.at[0, pl.ds(0, cut)], tf, far),
        "x0c0": (x_hbm.at[0], x0.at[pl.ds(pair, rows)], core),
        "x0fn": (tf, x0.at[pl.ds(rows, cut)], near),
        "x0nf": (tn, x0.at[pl.ds(rows + cut, cut)], far),
        "x0c1": (x0.at[pl.ds(rows, rows)], x0.at[pl.ds(pair + rows, rows)], core),
        "x1n": (x_hbm.at[1], xb.at[pl.ds(0, rows)], near),
        "x1f": (x_hbm.at[1], xb.at[pl.ds(rows, rows)], far),
        "x1c": (x_hbm.at[1], xa.at[pl.ds(pair, rows)], core),
        "x1fn": (xb.at[pl.ds(rows, cut)], xa.at[pl.ds(rows, cut)], near),
        "x1nf": (xb.at[pl.ds(cut, cut)], xa.at[pl.ds(rows + cut, cut)], far),
        "x1c1": (xa.at[pl.ds(rows, rows)], xa.at[pl.ds(pair + rows, rows)], core),
        "xbc": (xb.at[pl.ds(0, pair)], xb.at[pl.ds(pair, pair)], core),
        "xca": (x_hbm.at[1], xc.at[pl.ds(0, rows)], across),
        "xcb": (xa.at[pl.ds(rows, rows)], xc.at[pl.ds(rows, rows)], across),
        "xcc": (xc.at[pl.ds(0, pair)], xc.at[pl.ds(pair, pair)], core),
        "q": (q_give, q_got, near),
        "s1n": (s1, s1b, near),
        "s1x": (s1, s1c, across),
        "s1c": (s1.at[pl.ds(pair, pair)], s1o, core),
        "s1bc": (s1b.at[pl.ds(pair, pair)], s1bo, core),
        "st": (stepped, stepped_o, core),
        "p0c": (x0.at[pl.ds(pair, pair)], lp0, core),
        "a0f": (lp0.at[pl.ds(rows, cut)], t0f, far),
        "a0n": (lp0.at[pl.ds(rows + cut, cut)], t0n, near),
        "a0fn": (t0f, r0n, near),
        "a0nf": (t0n, r0f, far),
        "a1n": (xb.at[pl.ds(rows, cut)], t1n, near),
        "a1f": (xb.at[pl.ds(rows + cut, cut)], t1f, far),
        "to_near": (xb.at[pl.ds(pair, rows)], r1n, near),
        "to_far": (xb.at[pl.ds(pair + rows, rows)], r1f, far),
    }

    def copy(name):
        return remote(NUMBER[name], *routes[name])

    def go(*names):
        for name in names:
            copy(name).start()

    def arrived(*names):
        for name in names:
            copy(name).wait_recv()

    def sent(*names):
        for name in names:
            copy(name).wait_send()

    def link(name, i):
        here = piece(i * chunk, chunk)
        give = piece(give0 + i * chunk, chunk)
        src, dst, there = {
            "w1": (w_hbm.at[0, give], lw1.at[here], across),
            "w2": (lw1.at[here], lw2.at[here], near),
            "w3": (lw2.at[here], lw3.at[here], across),
            "m1": (mv.at[give], lm1.at[here], across),
            "m2": (lm1.at[here], lm2.at[here], near),
            "m3": (lm2.at[here], lm3.at[here], across),
        }[name]
        return remote(CHAINS[name] + i, src, dst, there)

    def load(k, src, dst):
        return pltpu.make_async_copy(src, dst, local.at[k])

    loads = [
        load(0, x_hbm.at[0], x0.at[pl.ds(0, rows)]),
        load(1, w_hbm.at[0], wv),
        load(2, og_hbm, og),
        load(3, x_hbm.at[1], xa.at[pl.ds(0, rows)]),
        load(4, m_hbm.at[0], mv),
    ]

    def each(count, body):
        @pl.loop(0, count)
        def _(i):
            body(i)

    loads[0].start()
    go("x0f", "x0n", "x0c0")
    loads[1].start()
    loads[2].start()
    each(CHUNKS, lambda i: link("w1", i).start())
    loads[4].start()
    loads[3].start()
    arrived("x0f")
    go("x0fn")
    arrived("x0n")
    go("x0nf", "x1n", "x1f", "x1c")
    arrived("x0fn", "x0nf")
    go("x0c1")
    loads[0].wait()
    loads[1].wait()
    loads[2].wait()
    arrived("x0c0", "x0c1")

    depth = d // 8

    def product(out, lhs, rhs):
        out[...] = jnp.zeros_like(out)

        def add(k):
            here = piece(k * depth, depth)
            out[...] += dot(lhs[:, here], rhs[here, :], 1, 0)

        each(d // depth, add)

    def slopes(out, step, pre):
        for j, block in enumerate((t, t_far, t_core, (t_core + 2) % 4)):
            up = og[step, piece(block * rows, rows), :].astype(f32)
            here = pl.ds(j * rows, rows)
            out[here, :] = (up * silu_slope(pre(here))).astype(bf16)

    product(q_own, x0, wv)
    slopes(s0, 0, lambda here: q_own[here, :])
    loads[4].wait()

    def moment_tile(start):
        here = piece(start, tile)
        grad = dot(x0[:, here], s0[...], 0, 0)
        moment = (mom_decay * mv[here, :].astype(f32) + grad).astype(bf16)
        mv[here, :] = moment
        stepped[here, :] = (wv[here, :].astype(f32) - learn_rate * moment.astype(f32)).astype(bf16)

    def moment_chunk(i):
        moment_tile(give0 + i * chunk)
        moment_tile(give0 + i * chunk + tile)
        link("m1", i).start()

    each(CHUNKS, moment_chunk)
    each(half // tile, lambda i: moment_tile(keep0 + i * tile))
    go("st")

    arrived("x1f")
    go("x1fn")
    arrived("x1n")
    go("x1nf")

    sent("x0c1")

    def part0(first):
        def one(k):
            here = piece(k * tile, tile)
            x0[pl.ds(first, pair), here] = dot(s0[pl.ds(first, pair), :], wv[here, :], 1, 1).astype(bf16)

        each(d // tile, one)

    part0(pair)
    go("p0c")
    part0(0)

    def pair_chunk(own, landed, first, second, i):
        link(first, i).wait_recv()
        here = piece(i * chunk, chunk)
        mine = own[piece(keep0 + i * chunk, chunk), :].astype(f32)
        landed[here, :] = ((mine + landed[here, :].astype(f32)) * 0.5).astype(bf16)
        link(second, i).start()

    def mean_chunk(landed, other, second, third, i):
        link(second, i).wait_recv()
        here = piece(i * chunk, chunk)
        other[here, :] = ((landed[here, :].astype(f32) + other[here, :].astype(f32)) * 0.5).astype(bf16)
        link(third, i).start()

    each(CHUNKS // 2, lambda i: pair_chunk(wv, lw1, "w1", "w2", i))

    loads[3].wait()
    arrived("x1fn", "x1nf")
    go("x1c1", "xbc")
    arrived("p0c")
    lp0[pl.ds(rows, rows), :] = (
        x0[pl.ds(rows, rows), :].astype(f32) + lp0[pl.ds(rows, rows), :].astype(f32)
    ).astype(bf16)
    go("a0f", "a0n")

    arrived("x1c", "x1c1", "xbc")
    product(q_give, xb, stepped)
    go("q")
    product(q_own, xa, stepped)
    go("xca")
    arrived("a0f")
    go("a0fn")
    arrived("a0n")
    go("a0nf")
    each(CHUNKS // 2, lambda i: pair_chunk(wv, lw1, "w1", "w2", i + CHUNKS // 2))
    arrived("q")
    slopes(s1, 1, lambda here: (q_own[here, :] + q_got[here, :]) * 0.5)
    go("s1c", "s1n", "s1x", "xcb")
    each(CHUNKS, lambda i: pair_chunk(mv, lm1, "m1", "m2", i))
    arrived("s1n")
    go("s1bc")
    arrived("s1c", "s1bc", "st")

    sent("x1fn", "x1nf", "xbc")

    def part1(k):
        here = piece(k * tile, tile)
        mine = jnp.concatenate([s1[pl.ds(0, pair), :], s1b[pl.ds(0, pair), :]], axis=0)
        theirs = jnp.concatenate([s1o[...], s1bo[...]], axis=0)
        both = dot(mine, stepped[here, :], 1, 1) + dot(theirs, stepped_o[here, :], 1, 1)
        xb[:, here] = (both * 0.5).astype(bf16)

    each(d // tile, part1)
    go("a1n", "a1f")

    each(CHUNKS, lambda i: mean_chunk(lw1, lw2, "w2", "w3", i))
    arrived("a1n")
    here = pl.ds(pair + rows, cut)
    xb[here, :] = (xb[here, :].astype(f32) + t1n[...].astype(f32)).astype(bf16)
    go("to_far")
    arrived("a1f")
    here = pl.ds(pair + cut, cut)
    xb[here, :] = (xb[here, :].astype(f32) + t1f[...].astype(f32)).astype(bf16)
    go("to_near")
    arrived("xca", "xcb")
    go("xcc")
    each(CHUNKS, lambda i: mean_chunk(lm1, lm2, "m2", "m3", i))

    arrived("a0fn", "a0nf")
    for k, back in enumerate((r0n, r0f)):
        here = pl.ds(k * cut, cut)
        x0[here, :] = (
            x0[here, :].astype(f32) + lp0[here, :].astype(f32) + back[...].astype(f32)
        ).astype(bf16)
    load(0, x0.at[pl.ds(0, rows)], grad_in.at[0]).start()

    arrived("s1x", "xcc")
    each(CHUNKS, lambda i: link("m1", i).wait_send())

    def finish(w_mean, m_mean, start, i):
        from_ = piece(i * tile, tile)
        here = piece(start + i * tile, tile)
        grad = dot(xa[:, here], s1[...], 0, 0) + dot(xc[:, here], s1c[...], 0, 0)
        m_now = m_mean[from_, :].astype(f32)
        moment = (mom_decay * m_now + grad * 0.5).astype(bf16)
        mv[here, :] = moment
        wv[here, :] = (
            w_mean[from_, :].astype(f32) - learn_rate * (m_now + moment.astype(f32))
        ).astype(bf16)

    each(half // tile, lambda i: finish(lw2, lm2, keep0, i))
    load(1, wv.at[piece(keep0, half)], new_w.at[0, piece(keep0, half)]).start()
    load(2, mv.at[piece(keep0, half)], new_m.at[0, piece(keep0, half)]).start()

    arrived("to_near", "to_far")
    x_first = xb[pl.ds(0, rows), :].astype(f32)
    xb[pl.ds(0, rows), :] = (x_first + r1n[...].astype(f32) + r1f[...].astype(f32)).astype(bf16)
    load(3, xb.at[pl.ds(0, rows)], grad_in.at[1]).start()

    def last_w(i):
        there = piece(give0 + i * chunk, chunk)
        return load(5 + i, wv.at[there], new_w.at[0, there])

    def last_m(i):
        there = piece(give0 + i * chunk, chunk)
        return load(5 + CHUNKS + i, mv.at[there], new_m.at[0, there])

    def finish_chunk(i):
        link("w3", i).wait_recv()
        link("m3", i).wait_recv()
        finish(lw3, lm3, give0, 2 * i)
        finish(lw3, lm3, give0, 2 * i + 1)
        last_w(i).start()
        last_m(i).start()

    each(CHUNKS, finish_chunk)

    sent(*[name for name in TRANSFERS if name not in ("x0c1", "x1fn", "x1nf", "xbc")])

    def drain(i):
        for name in ("w1", "w2", "w3", "m2", "m3"):
            link(name, i).wait_send()
        last_w(i).wait()
        last_m(i).wait()

    each(CHUNKS, drain)
    load(0, x0.at[pl.ds(0, rows)], grad_in.at[0]).wait()
    load(1, wv.at[piece(keep0, half)], new_w.at[0, piece(keep0, half)]).wait()
    load(2, mv.at[piece(keep0, half)], new_m.at[0, piece(keep0, half)]).wait()
    load(3, xb.at[pl.ds(0, rows)], grad_in.at[1]).wait()


def local(weight, momentum, inputs, out_grads):
    d, cols = weight.shape[1:]
    rows = inputs.shape[1]
    n, pair, cut, half = 4 * rows, 2 * rows, rows // 2, d // 2
    full = (d, cols)
    vmem = (
        [(full, bf16)] * 4
        + [((n, d), bf16)] * 4
        + [((half, cols), bf16)] * 6
        + [((cut, d), bf16)] * 2
        + [((pair, d), bf16)]
        + [((cut, d), bf16)] * 6
        + [((rows, d), bf16)] * 2
        + [((n, cols), f32)] * 3
        + [((2, n, cols), bf16)]
        + [((n, cols), bf16)] * 4
        + [((pair, cols), bf16)] * 2
    )
    return pl.pallas_call(
        kernel,
        out_shape=(
            jax.ShapeDtypeStruct(weight.shape, bf16),
            jax.ShapeDtypeStruct(momentum.shape, bf16),
            jax.ShapeDtypeStruct(inputs.shape, bf16),
        ),
        in_specs=[pl.BlockSpec(memory_space=pl.ANY)] * 4,
        out_specs=[pl.BlockSpec(memory_space=pl.ANY)] * 3,
        scratch_shapes=[pltpu.VMEM(shape, kind) for shape, kind in vmem]
        + [
            pltpu.SemaphoreType.DMA((COPIES,)),
            pltpu.SemaphoreType.DMA((COPIES,)),
            pltpu.SemaphoreType.DMA((5 + 2 * CHUNKS,)),
        ],
        compiler_params=pltpu.CompilerParams(
            collective_id=0, has_side_effects=True, vmem_limit_bytes=63 << 20
        ),
    )(weight, momentum, inputs, out_grads)


def solution(mesh):
    return jax.shard_map(
        local,
        mesh=mesh,
        in_specs=(
            P("replica", None, "tensor"),
            P("replica", None, "tensor"),
            P(None, ("replica", "tensor"), None),
            P(None, "replica", "tensor"),
        ),
        out_specs=(
            P("replica", None, "tensor"),
            P("replica", None, "tensor"),
            P(None, ("replica", "tensor"), None),
        ),
        check_vma=False,
    )
```

```python
import jax
import jax.numpy as jnp
from jax import lax
from jax.experimental import pallas as pl
from jax.experimental.pallas import tpu as pltpu
from jax.sharding import PartitionSpec as P

learn_rate = 0.001
mom_decay = 0.9

bf16 = jnp.bfloat16
f32 = jnp.float32

CHUNKS = 8
TRANSFERS = (
    "x0n0", "x0n1", "x0f0", "x0f1", "x0c0", "x0fn0", "x0fn1", "x0nf0", "x0nf1", "x0c1", "x1n",
    "x1f", "x1c", "x1fn", "x1nf", "x1c1", "xbc", "xca", "xcb", "xcd", "xcc", "q", "s1n", "s1x",
    "s1c", "s1bc", "st", "p0c", "a0f", "a0n", "a0fn", "a0nf", "a1n", "a1f", "to_near", "to_far",
)
NUMBER = {name: k for k, name in enumerate(TRANSFERS)}
CHAINS = {name: len(TRANSFERS) + CHUNKS * k for k, name in enumerate(("w1", "w2", "w3", "m1", "m2", "m3"))}
COPIES = len(TRANSFERS) + CHUNKS * len(CHAINS)


def silu_slope(pre):
    sigma = jax.nn.sigmoid(pre)
    return sigma * (1.0 + pre * (1.0 - sigma))


def dot(a, b, left, right):
    return lax.dot_general(a, b, (((left,), (right,)), ((), ())), preferred_element_type=f32)


def kernel(
    w_hbm, m_hbm, x_hbm, og_hbm, new_w, new_m, grad_in,
    wv, mv, stepped, stepped_o, x0, xa, xb, xc, lw1, lw2, lw3, lm1, lm2, lm3,
    tn, tf, lp0, t0n, t0f, r0n, r0f, t1n, t1f, r1n, r1f,
    q_own, q_give, q_got, og, s0, s1, s1b, s1c, s1o, s1bo,
    send, recv, local,
):
    d, cols = wv.shape
    rows = x0.shape[0] // 4
    cut = rows // 2
    half = d // 2
    chunk = half // CHUNKS
    piece_rows = cut // 2
    most = rows - cut // 2
    pair = 2 * rows

    r = lax.axis_index("replica")
    t = lax.axis_index("tensor")
    lower = (r // 2) % 2
    keep0 = lower * half
    give0 = (1 - lower) * half
    r_near = r + 1 - 2 * (r % 2)
    t_core = t + 1 - 2 * (t % 2)
    t_far = (t + 2) % 4
    core = (r, t_core)
    near = (r_near, t)
    far = (r_near, t_far)
    across = (r + 2 - 4 * lower, t)
    beyond = (r, t_far)

    barrier = pltpu.get_barrier_semaphore()
    for there in (core, near, far, across, beyond):
        pl.semaphore_signal(barrier, inc=1, device_id=there, device_id_type=pl.DeviceIdType.MESH)
    pl.semaphore_wait(barrier, 5)

    def piece(start, size):
        return pl.ds(pl.multiple_of(start, size), size)

    def remote(k, src, dst, there):
        return pltpu.make_async_remote_copy(
            src_ref=src, dst_ref=dst, send_sem=send.at[k], recv_sem=recv.at[k],
            device_id=there, device_id_type=pl.DeviceIdType.MESH,
        )

    routes = {
        "x0n0": (x_hbm.at[0, pl.ds(cut, piece_rows)], tn.at[pl.ds(0, piece_rows)], near),
        "x0n1": (x_hbm.at[0, pl.ds(most, piece_rows)], tn.at[pl.ds(piece_rows, piece_rows)], near),
        "x0f0": (x_hbm.at[0, pl.ds(0, piece_rows)], tf.at[pl.ds(0, piece_rows)], far),
        "x0f1": (x_hbm.at[0, pl.ds(piece_rows, piece_rows)], tf.at[pl.ds(piece_rows, piece_rows)], far),
        "x0c0": (x_hbm.at[0], x0.at[pl.ds(pair, rows)], core),
        "x0fn0": (tf.at[pl.ds(0, piece_rows)], x0.at[pl.ds(rows, piece_rows)], near),
        "x0fn1": (tf.at[pl.ds(piece_rows, piece_rows)], x0.at[pl.ds(rows + piece_rows, piece_rows)], near),
        "x0nf0": (tn.at[pl.ds(0, piece_rows)], x0.at[pl.ds(rows + cut, piece_rows)], far),
        "x0nf1": (tn.at[pl.ds(piece_rows, piece_rows)], x0.at[pl.ds(rows + most, piece_rows)], far),
        "x0c1": (x0.at[pl.ds(rows, rows)], x0.at[pl.ds(pair + rows, rows)], core),
        "x1n": (x_hbm.at[1], xb.at[pl.ds(0, rows)], near),
        "x1f": (x_hbm.at[1], xb.at[pl.ds(rows, rows)], far),
        "x1c": (x_hbm.at[1], xa.at[pl.ds(pair, rows)], core),
        "x1fn": (xb.at[pl.ds(rows, cut)], xa.at[pl.ds(rows, cut)], near),
        "x1nf": (xb.at[pl.ds(cut, cut)], xa.at[pl.ds(rows + cut, cut)], far),
        "x1c1": (xa.at[pl.ds(rows, rows)], xa.at[pl.ds(pair + rows, rows)], core),
        "xbc": (xb.at[pl.ds(0, pair)], xb.at[pl.ds(pair, pair)], core),
        "xca": (x_hbm.at[1], xc.at[pl.ds(0, rows)], across),
        "xcb": (xa.at[pl.ds(rows, most)], xc.at[pl.ds(rows, most)], across),
        "xcd": (xc.at[pl.ds(most, piece_rows)], xc.at[pl.ds(rows + most, piece_rows)], beyond),
        "xcc": (xc.at[pl.ds(0, pair)], xc.at[pl.ds(pair, pair)], core),
        "q": (q_give, q_got, near),
        "s1n": (s1, s1b, near),
        "s1x": (s1, s1c, across),
        "s1c": (s1.at[pl.ds(pair, pair)], s1o, core),
        "s1bc": (s1b.at[pl.ds(pair, pair)], s1bo, core),
        "st": (stepped, stepped_o, core),
        "p0c": (x0.at[pl.ds(pair, pair)], lp0, core),
        "a0f": (lp0.at[pl.ds(rows, cut)], t0f, far),
        "a0n": (lp0.at[pl.ds(rows + cut, cut)], t0n, near),
        "a0fn": (t0f, r0n, near),
        "a0nf": (t0n, r0f, far),
        "a1n": (xb.at[pl.ds(rows, cut)], t1n, near),
        "a1f": (xb.at[pl.ds(rows + cut, cut)], t1f, far),
        "to_near": (xb.at[pl.ds(pair, rows)], r1n, near),
        "to_far": (xb.at[pl.ds(pair + rows, rows)], r1f, far),
    }

    def copy(name):
        return remote(NUMBER[name], *routes[name])

    def go(*names):
        for name in names:
            copy(name).start()

    def arrived(*names):
        for name in names:
            copy(name).wait_recv()

    def sent(*names):
        for name in names:
            copy(name).wait_send()

    def link(name, i):
        here = piece(i * chunk, chunk)
        give = piece(give0 + i * chunk, chunk)
        src, dst, there = {
            "w1": (w_hbm.at[0, give], lw1.at[here], across),
            "w2": (lw1.at[here], lw2.at[here], near),
            "w3": (lw2.at[here], lw3.at[here], across),
            "m1": (mv.at[give], lm1.at[here], across),
            "m2": (lm1.at[here], lm2.at[here], near),
            "m3": (lm2.at[here], lm3.at[here], across),
        }[name]
        return remote(CHAINS[name] + i, src, dst, there)

    def load(k, src, dst):
        return pltpu.make_async_copy(src, dst, local.at[k])

    loads = [
        load(0, x_hbm.at[0], x0.at[pl.ds(0, rows)]),
        load(1, w_hbm.at[0], wv),
        load(2, og_hbm, og),
        load(3, x_hbm.at[1], xa.at[pl.ds(0, rows)]),
        load(4, m_hbm.at[0], mv),
    ]

    def each(count, body):
        @pl.loop(0, count)
        def _(i):
            body(i)

    loads[0].start()
    go("x0f0", "x0n0", "x0f1", "x0n1", "x0c0")
    each(CHUNKS, lambda i: link("w1", i).start())
    for load_now in loads[1:]:
        load_now.start()
    for k in "01":
        arrived("x0f" + k)
        go("x0fn" + k)
        arrived("x0n" + k)
        go("x0nf" + k)
    go("x1n", "x1f", "x1c")
    loads[1].wait()

    def pair_chunk(own, landed, first, second, i):
        link(first, i).wait_recv()
        here = piece(i * chunk, chunk)
        mine = own[piece(keep0 + i * chunk, chunk), :].astype(f32)
        landed[here, :] = ((mine + landed[here, :].astype(f32)) * 0.5).astype(bf16)
        link(second, i).start()

    def mean_chunk(landed, other, second, third, i):
        link(second, i).wait_recv()
        here = piece(i * chunk, chunk)
        other[here, :] = ((landed[here, :].astype(f32) + other[here, :].astype(f32)) * 0.5).astype(bf16)
        link(third, i).start()

    pair_chunk(wv, lw1, "w1", "w2", 0)
    loads[0].wait()
    loads[2].wait()
    arrived("x0c0", "x0fn0", "x0fn1", "x0nf0", "x0nf1")
    go("x0c1")
    arrived("x0c1")

    depth = d // 8

    def product(out, lhs, rhs):
        out[...] = jnp.zeros_like(out)

        def add(k):
            here = piece(k * depth, depth)
            out[...] += dot(lhs[:, here], rhs[here, :], 1, 0)

        each(d // depth, add)

    def slopes(out, step, pre):
        for j, block in enumerate((t, t_far, t_core, (t_core + 2) % 4)):
            up = og[step, piece(block * rows, rows), :].astype(f32)
            here = pl.ds(j * rows, rows)
            out[here, :] = (up * silu_slope(pre(here))).astype(bf16)

    product(q_own, x0, wv)
    slopes(s0, 0, lambda here: q_own[here, :])
    loads[4].wait()

    def moment_tile(start):
        here = piece(start, chunk)
        grad = dot(x0[:, here], s0[...], 0, 0)
        moment = (mom_decay * mv[here, :].astype(f32) + grad).astype(bf16)
        mv[here, :] = moment
        stepped[here, :] = (wv[here, :].astype(f32) - learn_rate * moment.astype(f32)).astype(bf16)

    def moment_chunk(i):
        moment_tile(give0 + i * chunk)
        link("m1", i).start()

    each(CHUNKS, moment_chunk)
    each(CHUNKS, lambda i: moment_tile(keep0 + i * chunk))
    go("st", "xca")

    sent("x0c1")

    def part0(first):
        def one(k):
            here = piece(k * chunk, chunk)
            x0[pl.ds(first, pair), here] = dot(s0[pl.ds(first, pair), :], wv[here, :], 1, 1).astype(bf16)

        each(d // chunk, one)

    part0(pair)
    go("p0c")
    part0(0)

    arrived("x1f")
    go("x1fn")
    arrived("x1n")
    go("x1nf", "xbc")
    arrived("p0c")
    lp0[pl.ds(rows, rows), :] = (
        x0[pl.ds(rows, rows), :].astype(f32) + lp0[pl.ds(rows, rows), :].astype(f32)
    ).astype(bf16)

    arrived("xbc")
    product(q_own, xb, stepped)
    q_give[...] = q_own[...].astype(bf16)
    go("q")
    pair_chunk(wv, lw1, "w1", "w2", 1)
    loads[3].wait()
    arrived("x1fn", "x1nf")
    go("x1c1", "xcb")
    arrived("x1c", "x1c1")
    product(q_own, xa, stepped)
    arrived("q")
    slopes(s1, 1, lambda here: (q_own[here, :] + q_got[here, :].astype(f32)) * 0.5)
    go("s1n", "s1x", "s1c")
    each(CHUNKS - 2, lambda i: pair_chunk(wv, lw1, "w1", "w2", i + 2))
    arrived("s1n")
    go("s1bc")
    arrived("s1c", "s1bc", "st")

    sent("x1fn", "x1nf", "xbc")

    def part1(k):
        here = piece(k * chunk, chunk)
        mine = jnp.concatenate([s1[pl.ds(0, pair), :], s1b[pl.ds(0, pair), :]], axis=0)
        theirs = jnp.concatenate([s1o[...], s1bo[...]], axis=0)
        both = dot(mine, stepped[here, :], 1, 1) + dot(theirs, stepped_o[here, :], 1, 1)
        xb[:, here] = (both * 0.5).astype(bf16)

    each(d // chunk, part1)
    go("a1n", "a1f")

    each(CHUNKS, lambda i: pair_chunk(mv, lm1, "m1", "m2", i))
    each(CHUNKS, lambda i: mean_chunk(lw1, lw2, "w2", "w3", i))
    arrived("xca")
    go("xcd", "a0n", "a0f")
    arrived("a1n")
    here = pl.ds(pair + rows, cut)
    xb[here, :] = (xb[here, :].astype(f32) + t1n[...].astype(f32)).astype(bf16)
    go("to_far")
    arrived("a1f")
    here = pl.ds(pair + cut, cut)
    xb[here, :] = (xb[here, :].astype(f32) + t1f[...].astype(f32)).astype(bf16)
    go("to_near")
    arrived("a0f")
    go("a0fn")
    each(CHUNKS, lambda i: mean_chunk(lm1, lm2, "m2", "m3", i))
    arrived("xcb", "xcd")
    go("xcc")
    arrived("a0n")
    go("a0nf")

    arrived("s1x", "xcc")
    each(CHUNKS, lambda i: link("m1", i).wait_send())

    def finish(w_mean, m_mean, start, i):
        from_ = piece(i * chunk, chunk)
        here = piece(start + i * chunk, chunk)
        grad = dot(xa[:, here], s1[...], 0, 0) + dot(xc[:, here], s1c[...], 0, 0)
        m_now = m_mean[from_, :].astype(f32)
        moment = (mom_decay * m_now + grad * 0.5).astype(bf16)
        mv[here, :] = moment
        wv[here, :] = (
            w_mean[from_, :].astype(f32) - learn_rate * (m_now + moment.astype(f32))
        ).astype(bf16)

    each(CHUNKS, lambda i: finish(lw2, lm2, keep0, i))
    load(1, wv.at[piece(keep0, half)], new_w.at[0, piece(keep0, half)]).start()
    load(2, mv.at[piece(keep0, half)], new_m.at[0, piece(keep0, half)]).start()

    def last_w(i):
        there = piece(give0 + i * chunk, chunk)
        return load(5 + i, wv.at[there], new_w.at[0, there])

    def last_m(i):
        there = piece(give0 + i * chunk, chunk)
        return load(5 + CHUNKS + i, mv.at[there], new_m.at[0, there])

    def finish_chunk(i):
        link("w3", i).wait_recv()
        link("m3", i).wait_recv()
        finish(lw3, lm3, give0, i)
        last_w(i).start()
        last_m(i).start()

    each(CHUNKS - 1, finish_chunk)

    arrived("a0fn", "a0nf")
    for k, back in enumerate((r0n, r0f)):
        here = pl.ds(k * cut, cut)
        x0[here, :] = (
            x0[here, :].astype(f32) + lp0[here, :].astype(f32) + back[...].astype(f32)
        ).astype(bf16)
    load(0, x0.at[pl.ds(0, rows)], grad_in.at[0]).start()
    arrived("to_near", "to_far")
    x_first = xb[pl.ds(0, rows), :].astype(f32)
    xb[pl.ds(0, rows), :] = (x_first + r1n[...].astype(f32) + r1f[...].astype(f32)).astype(bf16)
    load(3, xb.at[pl.ds(0, rows)], grad_in.at[1]).start()
    finish_chunk(CHUNKS - 1)

    sent(*[name for name in TRANSFERS if name not in ("x0c1", "x1fn", "x1nf", "xbc")])

    def drain(i):
        for name in ("w1", "w2", "w3", "m2", "m3"):
            link(name, i).wait_send()
        last_w(i).wait()
        last_m(i).wait()

    each(CHUNKS, drain)
    load(0, x0.at[pl.ds(0, rows)], grad_in.at[0]).wait()
    load(1, wv.at[piece(keep0, half)], new_w.at[0, piece(keep0, half)]).wait()
    load(2, mv.at[piece(keep0, half)], new_m.at[0, piece(keep0, half)]).wait()
    load(3, xb.at[pl.ds(0, rows)], grad_in.at[1]).wait()


def local(weight, momentum, inputs, out_grads):
    d, cols = weight.shape[1:]
    rows = inputs.shape[1]
    n, pair, cut, half = 4 * rows, 2 * rows, rows // 2, d // 2
    full = (d, cols)
    vmem = (
        [(full, bf16)] * 4
        + [((n, d), bf16)] * 4
        + [((half, cols), bf16)] * 6
        + [((cut, d), bf16)] * 2
        + [((pair, d), bf16)]
        + [((cut, d), bf16)] * 6
        + [((rows, d), bf16)] * 2
        + [((n, cols), f32)]
        + [((n, cols), bf16)] * 2
        + [((2, n, cols), bf16)]
        + [((n, cols), bf16)] * 4
        + [((pair, cols), bf16)] * 2
    )
    return pl.pallas_call(
        kernel,
        out_shape=(
            jax.ShapeDtypeStruct(weight.shape, bf16),
            jax.ShapeDtypeStruct(momentum.shape, bf16),
            jax.ShapeDtypeStruct(inputs.shape, bf16),
        ),
        in_specs=[pl.BlockSpec(memory_space=pl.ANY)] * 4,
        out_specs=[pl.BlockSpec(memory_space=pl.ANY)] * 3,
        scratch_shapes=[pltpu.VMEM(shape, kind) for shape, kind in vmem]
        + [
            pltpu.SemaphoreType.DMA((COPIES,)),
            pltpu.SemaphoreType.DMA((COPIES,)),
            pltpu.SemaphoreType.DMA((5 + 2 * CHUNKS,)),
        ],
        compiler_params=pltpu.CompilerParams(
            collective_id=0, has_side_effects=True, vmem_limit_bytes=63 << 20
        ),
    )(weight, momentum, inputs, out_grads)


def solution(mesh):
    return jax.shard_map(
        local,
        mesh=mesh,
        in_specs=(
            P("replica", None, "tensor"),
            P("replica", None, "tensor"),
            P(None, ("replica", "tensor"), None),
            P(None, "replica", "tensor"),
        ),
        out_specs=(
            P("replica", None, "tensor"),
            P("replica", None, "tensor"),
            P(None, ("replica", "tensor"), None),
        ),
        check_vma=False,
    )
```

```python
import jax
import jax.numpy as jnp
from jax import lax
from jax.experimental import pallas as pl
from jax.experimental.pallas import tpu as pltpu
from jax.sharding import PartitionSpec as P

learn_rate = 0.001
mom_decay = 0.9

bf16 = jnp.bfloat16
f32 = jnp.float32

CHUNKS = 8
TRANSFERS = (
    "x0n0", "x0n1", "x0f0", "x0f1", "x0c0", "x0fn0", "x0fn1", "x0nf0", "x0nf1", "x0c1", "x1n0",
    "x1n1", "x1f", "x1c", "x1nf0", "x1nf1", "x1c1", "xbc", "xca", "xcb", "xcd", "xcc", "q", "s1n",
    "s1x", "s1c", "s1bc", "st", "p0c", "a0f", "a0n", "a0fn", "a0nf", "a1f", "to_near", "to_far",
)
NUMBER = {name: k for k, name in enumerate(TRANSFERS)}
CHAINS = {name: len(TRANSFERS) + CHUNKS * k for k, name in enumerate(("w1", "w2", "w3", "m1", "m2", "m3"))}
COPIES = len(TRANSFERS) + CHUNKS * len(CHAINS)


def silu_slope(pre):
    sigma = jax.nn.sigmoid(pre)
    return sigma * (1.0 + pre * (1.0 - sigma))


def dot(a, b, left, right):
    return lax.dot_general(a, b, (((left,), (right,)), ((), ())), preferred_element_type=f32)


def kernel(
    w_hbm, m_hbm, x_hbm, og_hbm, new_w, new_m, grad_in,
    wv, mv, stepped, stepped_o, x0, xa, xb, xc, lw1, lw2, lw3, lm1, lm2, lm3,
    tn, tf, lp0, t0n, t0f, r0n, r0f, t1f, r1n, r1f,
    q_own, q_give, q_got, og, s0, s1, s1b, s1c, s1o, s1bo,
    send, recv, local,
):
    d, cols = wv.shape
    rows = x0.shape[0] // 4
    cut = rows // 2
    half = d // 2
    chunk = half // CHUNKS
    piece_rows = cut // 2
    most = rows - cut // 2
    pair = 2 * rows

    r = lax.axis_index("replica")
    t = lax.axis_index("tensor")
    lower = (r // 2) % 2
    keep0 = lower * half
    give0 = (1 - lower) * half
    r_near = r + 1 - 2 * (r % 2)
    t_core = t + 1 - 2 * (t % 2)
    t_far = (t + 2) % 4
    core = (r, t_core)
    near = (r_near, t)
    far = (r_near, t_far)
    across = (r + 2 - 4 * lower, t)
    beyond = (r, t_far)

    barrier = pltpu.get_barrier_semaphore()
    for there in (core, near, far, across, beyond):
        pl.semaphore_signal(barrier, inc=1, device_id=there, device_id_type=pl.DeviceIdType.MESH)
    pl.semaphore_wait(barrier, 5)

    def piece(start, size):
        return pl.ds(pl.multiple_of(start, size), size)

    def remote(k, src, dst, there):
        return pltpu.make_async_remote_copy(
            src_ref=src, dst_ref=dst, send_sem=send.at[k], recv_sem=recv.at[k],
            device_id=there, device_id_type=pl.DeviceIdType.MESH,
        )

    routes = {
        "x0n0": (x_hbm.at[0, pl.ds(cut, piece_rows)], tn.at[pl.ds(0, piece_rows)], near),
        "x0n1": (x_hbm.at[0, pl.ds(most, piece_rows)], tn.at[pl.ds(piece_rows, piece_rows)], near),
        "x0f0": (x_hbm.at[0, pl.ds(0, piece_rows)], tf.at[pl.ds(0, piece_rows)], far),
        "x0f1": (x_hbm.at[0, pl.ds(piece_rows, piece_rows)], tf.at[pl.ds(piece_rows, piece_rows)], far),
        "x0c0": (x_hbm.at[0], x0.at[pl.ds(pair, rows)], core),
        "x0fn0": (tf.at[pl.ds(0, piece_rows)], x0.at[pl.ds(rows, piece_rows)], near),
        "x0fn1": (tf.at[pl.ds(piece_rows, piece_rows)], x0.at[pl.ds(rows + piece_rows, piece_rows)], near),
        "x0nf0": (tn.at[pl.ds(0, piece_rows)], x0.at[pl.ds(rows + cut, piece_rows)], far),
        "x0nf1": (tn.at[pl.ds(piece_rows, piece_rows)], x0.at[pl.ds(rows + most, piece_rows)], far),
        "x0c1": (x0.at[pl.ds(rows, rows)], x0.at[pl.ds(pair + rows, rows)], core),
        "x1n0": (x_hbm.at[1, pl.ds(0, cut)], xb.at[pl.ds(0, cut)], near),
        "x1n1": (x_hbm.at[1, pl.ds(cut, cut)], xb.at[pl.ds(cut, cut)], near),
        "x1f": (x_hbm.at[1], xb.at[pl.ds(rows, rows)], far),
        "x1c": (x_hbm.at[1], xa.at[pl.ds(pair, rows)], core),
        "x1nf0": (xb.at[pl.ds(0, cut)], xa.at[pl.ds(rows, cut)], far),
        "x1nf1": (xb.at[pl.ds(cut, cut)], xa.at[pl.ds(rows + cut, cut)], far),
        "x1c1": (xa.at[pl.ds(rows, rows)], xa.at[pl.ds(pair + rows, rows)], core),
        "xbc": (xb.at[pl.ds(0, pair)], xb.at[pl.ds(pair, pair)], core),
        "xca": (x_hbm.at[1], xc.at[pl.ds(0, rows)], across),
        "xcb": (xa.at[pl.ds(rows, piece_rows)], xc.at[pl.ds(rows, piece_rows)], across),
        "xcd": (xc.at[pl.ds(piece_rows, most)], xc.at[pl.ds(rows + piece_rows, most)], beyond),
        "xcc": (xc.at[pl.ds(0, pair)], xc.at[pl.ds(pair, pair)], core),
        "q": (q_give, q_got, near),
        "s1n": (s1, s1b, near),
        "s1x": (s1, s1c, across),
        "s1c": (s1.at[pl.ds(pair, pair)], s1o, core),
        "s1bc": (s1b.at[pl.ds(pair, pair)], s1bo, core),
        "st": (stepped, stepped_o, core),
        "p0c": (x0.at[pl.ds(pair, pair)], lp0, core),
        "a0f": (lp0.at[pl.ds(rows, cut)], t0f, far),
        "a0n": (lp0.at[pl.ds(rows + cut, cut)], t0n, near),
        "a0fn": (t0f, r0n, near),
        "a0nf": (t0n, r0f, far),
        "a1f": (xb.at[pl.ds(rows, rows)], t1f, far),
        "to_near": (xb.at[pl.ds(pair, rows)], r1n, near),
        "to_far": (xb.at[pl.ds(pair + rows, rows)], r1f, far),
    }

    def copy(name):
        return remote(NUMBER[name], *routes[name])

    def go(*names):
        for name in names:
            copy(name).start()

    def arrived(*names):
        for name in names:
            copy(name).wait_recv()

    def sent(*names):
        for name in names:
            copy(name).wait_send()

    def link(name, i):
        here = piece(i * chunk, chunk)
        give = piece(give0 + i * chunk, chunk)
        src, dst, there = {
            "w1": (w_hbm.at[0, give], lw1.at[here], across),
            "w2": (lw1.at[here], lw2.at[here], near),
            "w3": (lw2.at[here], lw3.at[here], across),
            "m1": (mv.at[give], lm1.at[here], across),
            "m2": (lm1.at[here], lm2.at[here], near),
            "m3": (lm2.at[here], lm3.at[here], across),
        }[name]
        return remote(CHAINS[name] + i, src, dst, there)

    def load(k, src, dst):
        return pltpu.make_async_copy(src, dst, local.at[k])

    loads = [
        load(0, x_hbm.at[0], x0.at[pl.ds(0, rows)]),
        load(1, w_hbm.at[0], wv),
        load(2, og_hbm, og),
        load(3, x_hbm.at[1], xa.at[pl.ds(0, rows)]),
        load(4, m_hbm.at[0], mv),
    ]

    def each(count, body):
        @pl.loop(0, count)
        def _(i):
            body(i)

    loads[0].start()
    go("x0f0", "x0n0", "x0f1", "x0n1", "x0c0")
    each(CHUNKS, lambda i: link("w1", i).start())
    for load_now in loads[1:]:
        load_now.start()
    for k in "01":
        arrived("x0f" + k)
        go("x0fn" + k)
        arrived("x0n" + k)
        go("x0nf" + k)
    go("x1n0", "x1n1", "x1f", "x1c")
    loads[1].wait()

    def pair_chunk(own, landed, first, second, i):
        link(first, i).wait_recv()
        here = piece(i * chunk, chunk)
        mine = own[piece(keep0 + i * chunk, chunk), :].astype(f32)
        landed[here, :] = ((mine + landed[here, :].astype(f32)) * 0.5).astype(bf16)
        link(second, i).start()

    def mean_chunk(landed, other, second, third, i):
        link(second, i).wait_recv()
        here = piece(i * chunk, chunk)
        other[here, :] = ((landed[here, :].astype(f32) + other[here, :].astype(f32)) * 0.5).astype(bf16)
        link(third, i).start()

    each(2, lambda i: pair_chunk(wv, lw1, "w1", "w2", i))
    loads[0].wait()
    loads[2].wait()
    arrived("x0c0", "x0fn0", "x0fn1", "x0nf0", "x0nf1")
    go("x0c1")
    arrived("x0c1")

    depth = d // 8

    def product(out, lhs, rhs):
        out[...] = jnp.zeros_like(out)

        def add(k):
            here = piece(k * depth, depth)
            out[...] += dot(lhs[:, here], rhs[here, :], 1, 0)

        each(d // depth, add)

    def slopes(out, step, pre):
        for j, block in enumerate((t, t_far, t_core, (t_core + 2) % 4)):
            up = og[step, piece(block * rows, rows), :].astype(f32)
            here = pl.ds(j * rows, rows)
            out[here, :] = (up * silu_slope(pre(here))).astype(bf16)

    product(q_own, x0, wv)
    slopes(s0, 0, lambda here: q_own[here, :])
    loads[4].wait()

    def moment_tile(start):
        here = piece(start, chunk)
        grad = dot(x0[:, here], s0[...], 0, 0)
        moment = (mom_decay * mv[here, :].astype(f32) + grad).astype(bf16)
        mv[here, :] = moment
        stepped[here, :] = (wv[here, :].astype(f32) - learn_rate * moment.astype(f32)).astype(bf16)

    def moment_chunk(i):
        moment_tile(give0 + i * chunk)
        link("m1", i).start()

    each(CHUNKS, moment_chunk)
    each(CHUNKS, lambda i: moment_tile(keep0 + i * chunk))
    go("st", "xca")

    sent("x0c1")
    arrived("x1n0")
    go("x1nf0")

    def part0(first):
        def one(k):
            here = piece(k * chunk, chunk)
            x0[pl.ds(first, pair), here] = dot(s0[pl.ds(first, pair), :], wv[here, :], 1, 1).astype(bf16)

        each(d // chunk, one)

    part0(pair)
    go("p0c")
    part0(0)

    arrived("x1n1")
    go("x1nf1")
    arrived("x1f")
    go("xbc")
    arrived("p0c")
    lp0[pl.ds(rows, rows), :] = (
        x0[pl.ds(rows, rows), :].astype(f32) + lp0[pl.ds(rows, rows), :].astype(f32)
    ).astype(bf16)

    arrived("xbc")
    product(q_own, xb, stepped)
    q_give[...] = q_own[...].astype(bf16)
    go("q")
    each(2, lambda i: pair_chunk(wv, lw1, "w1", "w2", i + 2))
    loads[3].wait()
    arrived("x1nf0", "x1nf1")
    go("x1c1", "xcb")
    arrived("x1c", "x1c1")
    product(q_own, xa, stepped)
    arrived("q")
    slopes(s1, 1, lambda here: (q_own[here, :] + q_got[here, :].astype(f32)) * 0.5)
    go("s1n", "s1x", "s1c")
    each(CHUNKS - 4, lambda i: pair_chunk(wv, lw1, "w1", "w2", i + 4))
    arrived("s1n")
    go("s1bc")
    arrived("s1c", "s1bc", "st")

    sent("x1nf0", "x1nf1", "xbc")

    def part1(k):
        here = piece(k * chunk, chunk)
        mine = jnp.concatenate([s1[pl.ds(0, pair), :], s1b[pl.ds(0, pair), :]], axis=0)
        theirs = jnp.concatenate([s1o[...], s1bo[...]], axis=0)
        both = dot(mine, stepped[here, :], 1, 1) + dot(theirs, stepped_o[here, :], 1, 1)
        xb[:, here] = (both * 0.5).astype(bf16)

    each(d // chunk, part1)
    go("a1f", "to_far")

    each(CHUNKS, lambda i: pair_chunk(mv, lm1, "m1", "m2", i))
    each(CHUNKS, lambda i: mean_chunk(lw1, lw2, "w2", "w3", i))
    arrived("xca")
    go("xcd", "a0n", "a0f")
    arrived("a1f")
    here = pl.ds(pair, rows)
    xb[here, :] = (xb[here, :].astype(f32) + t1f[...].astype(f32)).astype(bf16)
    go("to_near")
    arrived("a0f")
    go("a0fn")
    each(CHUNKS, lambda i: mean_chunk(lm1, lm2, "m2", "m3", i))
    arrived("xcb", "xcd")
    go("xcc")
    arrived("a0n")
    go("a0nf")

    arrived("s1x", "xcc")
    each(CHUNKS, lambda i: link("m1", i).wait_send())

    def finish(w_mean, m_mean, start, i):
        from_ = piece(i * chunk, chunk)
        here = piece(start + i * chunk, chunk)
        grad = dot(xa[:, here], s1[...], 0, 0) + dot(xc[:, here], s1c[...], 0, 0)
        m_now = m_mean[from_, :].astype(f32)
        moment = (mom_decay * m_now + grad * 0.5).astype(bf16)
        mv[here, :] = moment
        wv[here, :] = (
            w_mean[from_, :].astype(f32) - learn_rate * (m_now + moment.astype(f32))
        ).astype(bf16)

    each(CHUNKS, lambda i: finish(lw2, lm2, keep0, i))
    load(1, wv.at[piece(keep0, half)], new_w.at[0, piece(keep0, half)]).start()
    load(2, mv.at[piece(keep0, half)], new_m.at[0, piece(keep0, half)]).start()

    def last_w(i):
        there = piece(give0 + i * chunk, chunk)
        return load(5 + i, wv.at[there], new_w.at[0, there])

    def last_m(i):
        there = piece(give0 + i * chunk, chunk)
        return load(5 + CHUNKS + i, mv.at[there], new_m.at[0, there])

    def finish_chunk(i):
        link("w3", i).wait_recv()
        link("m3", i).wait_recv()
        finish(lw3, lm3, give0, i)
        last_w(i).start()
        last_m(i).start()

    each(CHUNKS - 1, finish_chunk)

    arrived("a0fn", "a0nf")
    for k, back in enumerate((r0n, r0f)):
        here = pl.ds(k * cut, cut)
        x0[here, :] = (
            x0[here, :].astype(f32) + lp0[here, :].astype(f32) + back[...].astype(f32)
        ).astype(bf16)
    load(0, x0.at[pl.ds(0, rows)], grad_in.at[0]).start()
    arrived("to_near", "to_far")
    x_first = xb[pl.ds(0, rows), :].astype(f32)
    xb[pl.ds(0, rows), :] = (x_first + r1n[...].astype(f32) + r1f[...].astype(f32)).astype(bf16)
    load(3, xb.at[pl.ds(0, rows)], grad_in.at[1]).start()
    finish_chunk(CHUNKS - 1)

    sent(*[name for name in TRANSFERS if name not in ("x0c1", "x1nf0", "x1nf1", "xbc")])

    def drain(i):
        for name in ("w1", "w2", "w3", "m2", "m3"):
            link(name, i).wait_send()
        last_w(i).wait()
        last_m(i).wait()

    each(CHUNKS, drain)
    load(0, x0.at[pl.ds(0, rows)], grad_in.at[0]).wait()
    load(1, wv.at[piece(keep0, half)], new_w.at[0, piece(keep0, half)]).wait()
    load(2, mv.at[piece(keep0, half)], new_m.at[0, piece(keep0, half)]).wait()
    load(3, xb.at[pl.ds(0, rows)], grad_in.at[1]).wait()


def local(weight, momentum, inputs, out_grads):
    d, cols = weight.shape[1:]
    rows = inputs.shape[1]
    n, pair, cut, half = 4 * rows, 2 * rows, rows // 2, d // 2
    full = (d, cols)
    vmem = (
        [(full, bf16)] * 4
        + [((n, d), bf16)] * 4
        + [((half, cols), bf16)] * 6
        + [((cut, d), bf16)] * 2
        + [((pair, d), bf16)]
        + [((cut, d), bf16)] * 4
        + [((rows, d), bf16)] * 3
        + [((n, cols), f32)]
        + [((n, cols), bf16)] * 2
        + [((2, n, cols), bf16)]
        + [((n, cols), bf16)] * 4
        + [((pair, cols), bf16)] * 2
    )
    return pl.pallas_call(
        kernel,
        out_shape=(
            jax.ShapeDtypeStruct(weight.shape, bf16),
            jax.ShapeDtypeStruct(momentum.shape, bf16),
            jax.ShapeDtypeStruct(inputs.shape, bf16),
        ),
        in_specs=[pl.BlockSpec(memory_space=pl.ANY)] * 4,
        out_specs=[pl.BlockSpec(memory_space=pl.ANY)] * 3,
        scratch_shapes=[pltpu.VMEM(shape, kind) for shape, kind in vmem]
        + [
            pltpu.SemaphoreType.DMA((COPIES,)),
            pltpu.SemaphoreType.DMA((COPIES,)),
            pltpu.SemaphoreType.DMA((5 + 2 * CHUNKS,)),
        ],
        compiler_params=pltpu.CompilerParams(
            collective_id=0, has_side_effects=True, vmem_limit_bytes=63 << 20
        ),
    )(weight, momentum, inputs, out_grads)


def solution(mesh):
    return jax.shard_map(
        local,
        mesh=mesh,
        in_specs=(
            P("replica", None, "tensor"),
            P("replica", None, "tensor"),
            P(None, ("replica", "tensor"), None),
            P(None, "replica", "tensor"),
        ),
        out_specs=(
            P("replica", None, "tensor"),
            P("replica", None, "tensor"),
            P(None, ("replica", "tensor"), None),
        ),
        check_vma=False,
    )
```

```python
import jax
import jax.numpy as jnp
from jax import lax
from jax.experimental import pallas as pl
from jax.experimental.pallas import tpu as pltpu
from jax.sharding import PartitionSpec as P

learn_rate = 0.001
mom_decay = 0.9

bf16 = jnp.bfloat16
f32 = jnp.float32

CHUNKS = 8
TRANSFERS = (
    "x0n0", "x0n1", "x0f0", "x0f1", "x0c0", "x0fn0", "x0fn1", "x0nf0", "x0nf1", "x0c1", "x1n0",
    "x1n1", "x1f", "x1c", "x1nf0", "x1nf1", "x1c1", "xbc", "xca", "xcb", "xcd", "xcc", "q", "s1n",
    "s1x", "s1c", "s1bc", "st", "p0c", "a0f", "a0n", "a0fn", "a0nf", "a1f", "to_near", "to_far",
)
NUMBER = {name: k for k, name in enumerate(TRANSFERS)}
AWAITED = ("x0c1", "x1nf0", "x1nf1", "xbc", "x0fn0", "x0fn1", "x0nf0", "x0nf1", "p0c")
CHAINS = {name: len(TRANSFERS) + CHUNKS * k for k, name in enumerate(("w1", "w2", "w3", "m1", "m2", "m3"))}
COPIES = len(TRANSFERS) + CHUNKS * len(CHAINS)


def silu_slope(pre):
    sigma = jax.nn.sigmoid(pre)
    return sigma * (1.0 + pre * (1.0 - sigma))


def dot(a, b, left, right):
    return lax.dot_general(a, b, (((left,), (right,)), ((), ())), preferred_element_type=f32)


def kernel(
    w_hbm, m_hbm, x_hbm, og_hbm, new_w, new_m, grad_in,
    stepped, stepped_o, x0, xa, xb, xc, lw1, lw2, lw3, lm1, lm2, lm3,
    tn, tf, lp0, t1f, r1f, q_own, q_got, og, s0, s1b, s1c, s1o, s1bo,
    send, recv, local,
):
    wv, mv = new_w.at[0], new_m.at[0]
    d, cols = stepped.shape
    rows = x0.shape[0] // 4
    cut = rows // 2
    half = d // 2
    chunk = half // CHUNKS
    piece_rows = cut // 2
    most = rows - cut // 2
    pair = 2 * rows
    s1 = s0
    q_give = og.at[0]
    t0n, t0f = tn, tf
    r1n = x0.at[pl.ds(pair, rows)]
    r0n = x0.at[pl.ds(pair + rows, cut)]
    r0f = x0.at[pl.ds(pair + rows + cut, cut)]

    r = lax.axis_index("replica")
    t = lax.axis_index("tensor")
    lower = (r // 2) % 2
    keep0 = lower * half
    give0 = (1 - lower) * half
    r_near = r + 1 - 2 * (r % 2)
    t_core = t + 1 - 2 * (t % 2)
    t_far = (t + 2) % 4
    core = (r, t_core)
    near = (r_near, t)
    far = (r_near, t_far)
    across = (r + 2 - 4 * lower, t)
    beyond = (r, t_far)

    barrier = pltpu.get_barrier_semaphore()
    for there in (core, near, far, across, beyond):
        pl.semaphore_signal(barrier, inc=1, device_id=there, device_id_type=pl.DeviceIdType.MESH)
    pl.semaphore_wait(barrier, 5)

    def piece(start, size):
        return pl.ds(pl.multiple_of(start, size), size)

    def remote(k, src, dst, there):
        return pltpu.make_async_remote_copy(
            src_ref=src, dst_ref=dst, send_sem=send.at[k], recv_sem=recv.at[k],
            device_id=there, device_id_type=pl.DeviceIdType.MESH,
        )

    routes = {
        "x0n0": (x_hbm.at[0, pl.ds(cut, piece_rows)], tn.at[pl.ds(0, piece_rows)], near),
        "x0n1": (x_hbm.at[0, pl.ds(most, piece_rows)], tn.at[pl.ds(piece_rows, piece_rows)], near),
        "x0f0": (x_hbm.at[0, pl.ds(0, piece_rows)], tf.at[pl.ds(0, piece_rows)], far),
        "x0f1": (x_hbm.at[0, pl.ds(piece_rows, piece_rows)], tf.at[pl.ds(piece_rows, piece_rows)], far),
        "x0c0": (x_hbm.at[0], x0.at[pl.ds(pair, rows)], core),
        "x0fn0": (tf.at[pl.ds(0, piece_rows)], x0.at[pl.ds(rows, piece_rows)], near),
        "x0fn1": (tf.at[pl.ds(piece_rows, piece_rows)], x0.at[pl.ds(rows + piece_rows, piece_rows)], near),
        "x0nf0": (tn.at[pl.ds(0, piece_rows)], x0.at[pl.ds(rows + cut, piece_rows)], far),
        "x0nf1": (tn.at[pl.ds(piece_rows, piece_rows)], x0.at[pl.ds(rows + most, piece_rows)], far),
        "x0c1": (x0.at[pl.ds(rows, rows)], x0.at[pl.ds(pair + rows, rows)], core),
        "x1n0": (x_hbm.at[1, pl.ds(0, cut)], xb.at[pl.ds(0, cut)], near),
        "x1n1": (x_hbm.at[1, pl.ds(cut, cut)], xb.at[pl.ds(cut, cut)], near),
        "x1f": (x_hbm.at[1], xb.at[pl.ds(rows, rows)], far),
        "x1c": (x_hbm.at[1], xa.at[pl.ds(pair, rows)], core),
        "x1nf0": (xb.at[pl.ds(0, cut)], xa.at[pl.ds(rows, cut)], far),
        "x1nf1": (xb.at[pl.ds(cut, cut)], xa.at[pl.ds(rows + cut, cut)], far),
        "x1c1": (xa.at[pl.ds(rows, rows)], xa.at[pl.ds(pair + rows, rows)], core),
        "xbc": (xb.at[pl.ds(0, pair)], xb.at[pl.ds(pair, pair)], core),
        "xca": (x_hbm.at[1], xc.at[pl.ds(0, rows)], across),
        "xcb": (xa.at[pl.ds(rows, piece_rows)], xc.at[pl.ds(rows, piece_rows)], across),
        "xcd": (xc.at[pl.ds(piece_rows, most)], xc.at[pl.ds(rows + piece_rows, most)], beyond),
        "xcc": (xc.at[pl.ds(0, pair)], xc.at[pl.ds(pair, pair)], core),
        "q": (q_give, q_got, near),
        "s1n": (s1, s1b, near),
        "s1x": (s1, s1c, across),
        "s1c": (s1.at[pl.ds(pair, pair)], s1o, core),
        "s1bc": (s1b.at[pl.ds(pair, pair)], s1bo, core),
        "st": (stepped, stepped_o, core),
        "p0c": (x0.at[pl.ds(pair, pair)], lp0, core),
        "a0f": (lp0.at[pl.ds(rows, cut)], t0f, far),
        "a0n": (lp0.at[pl.ds(rows + cut, cut)], t0n, near),
        "a0fn": (t0f, r0n, near),
        "a0nf": (t0n, r0f, far),
        "a1f": (xb.at[pl.ds(rows, rows)], t1f, far),
        "to_near": (xb.at[pl.ds(pair, rows)], r1n, near),
        "to_far": (xb.at[pl.ds(pair + rows, rows)], r1f, far),
    }

    def copy(name):
        return remote(NUMBER[name], *routes[name])

    def go(*names):
        for name in names:
            copy(name).start()

    def arrived(*names):
        for name in names:
            copy(name).wait_recv()

    def sent(*names):
        for name in names:
            copy(name).wait_send()

    def link(name, i):
        here = piece(i * chunk, chunk)
        give = piece(give0 + i * chunk, chunk)
        src, dst, there = {
            "w1": (w_hbm.at[0, give], lw1.at[here], across),
            "w2": (lw1.at[here], lw2.at[here], near),
            "w3": (lw2.at[here], lw3.at[here], across),
            "m1": (mv.at[give], lm1.at[here], across),
            "m2": (lm1.at[here], lm2.at[here], near),
            "m3": (lm2.at[here], lm3.at[here], across),
        }[name]
        return remote(CHAINS[name] + i, src, dst, there)

    def load(k, src, dst):
        return pltpu.make_async_copy(src, dst, local.at[k])

    loads = [
        load(0, x_hbm.at[0], x0.at[pl.ds(0, rows)]),
        load(1, w_hbm.at[0], wv),
        load(2, og_hbm, og),
        load(3, x_hbm.at[1], xa.at[pl.ds(0, rows)]),
        load(4, m_hbm.at[0], mv),
    ]

    def each(count, body):
        @pl.loop(0, count)
        def _(i):
            body(i)

    loads[0].start()
    go("x0f0", "x0n0", "x0f1", "x0n1", "x0c0")
    each(CHUNKS, lambda i: link("w1", i).start())
    for load_now in loads[1:]:
        load_now.start()
    for k in "01":
        arrived("x0f" + k)
        go("x0fn" + k)
        arrived("x0n" + k)
        go("x0nf" + k)
    go("x1n0", "x1n1", "x1f", "x1c")
    loads[1].wait()

    def pair_chunk(own, landed, first, second, i):
        link(first, i).wait_recv()
        here = piece(i * chunk, chunk)
        mine = own[piece(keep0 + i * chunk, chunk), :].astype(f32)
        landed[here, :] = ((mine + landed[here, :].astype(f32)) * 0.5).astype(bf16)
        link(second, i).start()

    def mean_chunk(landed, other, second, third, i):
        link(second, i).wait_recv()
        here = piece(i * chunk, chunk)
        other[here, :] = ((landed[here, :].astype(f32) + other[here, :].astype(f32)) * 0.5).astype(bf16)
        link(third, i).start()

    each(2, lambda i: pair_chunk(wv, lw1, "w1", "w2", i))
    loads[0].wait()
    loads[2].wait()
    arrived("x0c0", "x0fn0", "x0fn1", "x0nf0", "x0nf1")
    go("x0c1")
    arrived("x0c1")

    depth = d // 8

    def product(out, lhs, rhs):
        out[...] = jnp.zeros_like(out)

        def add(k):
            here = piece(k * depth, depth)
            out[...] += dot(lhs[:, here], rhs[here, :], 1, 0)

        each(d // depth, add)

    def slopes(out, step, pre):
        for j, block in enumerate((t, t_far, t_core, (t_core + 2) % 4)):
            up = og[step, piece(block * rows, rows), :].astype(f32)
            here = pl.ds(j * rows, rows)
            out[here, :] = (up * silu_slope(pre(here))).astype(bf16)

    product(q_own, x0, wv)
    slopes(s0, 0, lambda here: q_own[here, :])
    loads[4].wait()

    def moment_tile(start):
        here = piece(start, chunk)
        grad = dot(x0[:, here], s0[...], 0, 0)
        moment = (mom_decay * mv[here, :].astype(f32) + grad).astype(bf16)
        mv[here, :] = moment
        stepped[here, :] = (wv[here, :].astype(f32) - learn_rate * moment.astype(f32)).astype(bf16)

    def moment_chunk(i):
        moment_tile(give0 + i * chunk)
        link("m1", i).start()

    each(CHUNKS, moment_chunk)
    each(CHUNKS, lambda i: moment_tile(keep0 + i * chunk))
    go("st", "xca")

    sent("x0c1")
    arrived("x1n0")
    go("x1nf0")

    def part0(first):
        def one(k):
            here = piece(k * chunk, chunk)
            x0[pl.ds(first, pair), here] = dot(s0[pl.ds(first, pair), :], wv[here, :], 1, 1).astype(bf16)

        each(d // chunk, one)

    part0(pair)
    go("p0c")
    part0(0)

    arrived("x1n1")
    sent("x0fn0", "x0fn1", "x0nf0", "x0nf1")
    go("x1nf1")
    arrived("x1f")
    go("xbc")
    arrived("p0c")
    lp0[pl.ds(rows, rows), :] = (
        x0[pl.ds(rows, rows), :].astype(f32) + lp0[pl.ds(rows, rows), :].astype(f32)
    ).astype(bf16)

    arrived("xbc")
    product(q_own, xb, stepped)
    q_give[...] = q_own[...].astype(bf16)
    go("q")
    each(2, lambda i: pair_chunk(wv, lw1, "w1", "w2", i + 2))
    loads[3].wait()
    arrived("x1nf0", "x1nf1")
    go("x1c1", "xcb")
    arrived("x1c", "x1c1")
    product(q_own, xa, stepped)
    arrived("q")
    sent("p0c")
    slopes(s1, 1, lambda here: (q_own[here, :] + q_got[here, :].astype(f32)) * 0.5)
    go("s1n", "s1x", "s1c")
    each(CHUNKS - 4, lambda i: pair_chunk(wv, lw1, "w1", "w2", i + 4))
    arrived("s1n")
    go("s1bc")
    arrived("s1c", "s1bc", "st")

    sent("x1nf0", "x1nf1", "xbc")

    def part1(k):
        here = piece(k * chunk, chunk)
        mine = jnp.concatenate([s1[pl.ds(0, pair), :], s1b[pl.ds(0, pair), :]], axis=0)
        theirs = jnp.concatenate([s1o[...], s1bo[...]], axis=0)
        both = dot(mine, stepped[here, :], 1, 1) + dot(theirs, stepped_o[here, :], 1, 1)
        xb[:, here] = (both * 0.5).astype(bf16)

    each(d // chunk, part1)
    go("a1f", "to_far")

    each(CHUNKS, lambda i: pair_chunk(mv, lm1, "m1", "m2", i))
    each(CHUNKS, lambda i: mean_chunk(lw1, lw2, "w2", "w3", i))
    arrived("xca")
    go("xcd", "a0n", "a0f")
    arrived("a1f")
    here = pl.ds(pair, rows)
    xb[here, :] = (xb[here, :].astype(f32) + t1f[...].astype(f32)).astype(bf16)
    go("to_near")
    arrived("a0f")
    go("a0fn")
    each(CHUNKS, lambda i: mean_chunk(lm1, lm2, "m2", "m3", i))
    arrived("xcb", "xcd")
    go("xcc")
    arrived("a0n")
    go("a0nf")

    arrived("s1x", "xcc")
    each(CHUNKS, lambda i: link("m1", i).wait_send())

    def finish(w_mean, m_mean, start, i, wait):
        from_ = piece(i * chunk, chunk)
        here = piece(start + i * chunk, chunk)
        if wait:
            link("w3", i).wait_recv()
            link("m3", i).wait_recv()
        grad = dot(xa[:, here], s1[...], 0, 0) + dot(xc[:, here], s1c[...], 0, 0)
        m_now = m_mean[from_, :].astype(f32)
        moment = (mom_decay * m_now + grad * 0.5).astype(bf16)
        mv[here, :] = moment
        wv[here, :] = (
            w_mean[from_, :].astype(f32) - learn_rate * (m_now + moment.astype(f32))
        ).astype(bf16)

    each(CHUNKS, lambda i: finish(lw2, lm2, keep0, i, False))

    def finish_chunk(i):
        finish(lw3, lm3, give0, i, True)

    each(CHUNKS - 1, finish_chunk)

    arrived("a0fn", "a0nf")
    for k, back in enumerate((r0n, r0f)):
        here = pl.ds(k * cut, cut)
        grad_in[0, here, :] = (
            x0[here, :].astype(f32) + lp0[here, :].astype(f32) + back[...].astype(f32)
        ).astype(bf16)
    arrived("to_near", "to_far")
    x_first = xb[pl.ds(0, rows), :].astype(f32)
    grad_in[1, :, :] = (x_first + r1n[...].astype(f32) + r1f[...].astype(f32)).astype(bf16)
    finish_chunk(CHUNKS - 1)

    sent(*[name for name in TRANSFERS if name not in AWAITED])

    def drain(i):
        for name in ("w1", "w2", "w3", "m2", "m3"):
            link(name, i).wait_send()

    each(CHUNKS, drain)


def local(weight, momentum, inputs, out_grads):
    d, cols = weight.shape[1:]
    rows = inputs.shape[1]
    n, pair, cut, half = 4 * rows, 2 * rows, rows // 2, d // 2
    full = (d, cols)
    vmem = (
        [(full, bf16)] * 2
        + [((n, d), bf16)] * 4
        + [((half, cols), bf16)] * 6
        + [((cut, d), bf16)] * 2
        + [((pair, d), bf16)]
        + [((rows, d), bf16)] * 2
        + [((n, cols), f32)]
        + [((n, cols), bf16)]
        + [((2, n, cols), bf16)]
        + [((n, cols), bf16)] * 3
        + [((pair, cols), bf16)] * 2
    )
    return pl.pallas_call(
        kernel,
        out_shape=(
            pltpu.VMEM(weight.shape, bf16),
            pltpu.VMEM(momentum.shape, bf16),
            pltpu.VMEM(inputs.shape, bf16),
        ),
        in_specs=[pl.BlockSpec(memory_space=pl.ANY)] * 4,
        out_specs=[pl.BlockSpec(memory_space=pltpu.VMEM)] * 3,
        scratch_shapes=[pltpu.VMEM(shape, kind) for shape, kind in vmem]
        + [
            pltpu.SemaphoreType.DMA((COPIES,)),
            pltpu.SemaphoreType.DMA((COPIES,)),
            pltpu.SemaphoreType.DMA((5,)),
        ],
        compiler_params=pltpu.CompilerParams(
            collective_id=0, has_side_effects=True, vmem_limit_bytes=53 << 20
        ),
    )(weight, momentum, inputs, out_grads)


def solution(mesh):
    return jax.shard_map(
        local,
        mesh=mesh,
        in_specs=(
            P("replica", None, "tensor"),
            P("replica", None, "tensor"),
            P(None, ("replica", "tensor"), None),
            P(None, "replica", "tensor"),
        ),
        out_specs=(
            P("replica", None, "tensor"),
            P("replica", None, "tensor"),
            P(None, ("replica", "tensor"), None),
        ),
        check_vma=False,
    )
```

```python
import jax
import jax.numpy as jnp
from jax import lax
from jax.experimental import pallas as pl
from jax.experimental.pallas import tpu as pltpu
from jax.sharding import PartitionSpec as P

learn_rate = 0.001
mom_decay = 0.9

bf16 = jnp.bfloat16
f32 = jnp.float32

CHUNKS = 8
TRANSFERS = (
    "x0n0", "x0n1", "x0f0", "x0f1", "x0c0", "x0fn0", "x0fn1", "x0nf0", "x0nf1", "x0c1", "x1n0",
    "x1n1", "x1f", "x1c", "x1nf0", "x1nf1", "x1c1", "xbc", "xca", "xcb", "xcd", "xcc", "q", "s1n",
    "s1x", "s1c", "s1bc", "st", "p0c", "a0f", "a0n", "a0fn", "a0nf", "a1f", "to_near", "to_far",
)
NUMBER = {name: k for k, name in enumerate(TRANSFERS)}
AWAITED = ("x0c1", "x1nf0", "x1nf1", "xbc", "x0fn0", "x0fn1", "x0nf0", "x0nf1", "p0c")
CHAINS = {name: len(TRANSFERS) + CHUNKS * k for k, name in enumerate(("w1", "w2", "w3", "m1", "m2", "m3"))}
COPIES = len(TRANSFERS) + CHUNKS * len(CHAINS)


def silu_slope(pre):
    sigma = jax.nn.sigmoid(pre)
    return sigma * (1.0 + pre * (1.0 - sigma))


def dot(a, b, left, right):
    return lax.dot_general(a, b, (((left,), (right,)), ((), ())), preferred_element_type=f32)


def kernel(
    w_hbm, m_hbm, x_hbm, og_hbm, new_w, new_m, grad_in,
    stepped, stepped_o, x0, xa, xb, xc, lw1, lw2, lw3, lm1, lm2, lm3,
    tn, tf, lp0, t1f, r1f, q_own, q_got, og, s0, s1b, s1c, s1o, s1bo,
    send, recv, local,
):
    wv, mv = new_w.at[0], new_m.at[0]
    d, cols = stepped.shape
    rows = x0.shape[0] // 4
    cut = rows // 2
    half = d // 2
    chunk = half // CHUNKS
    piece_rows = cut // 2
    most = rows - cut // 2
    pair = 2 * rows
    s1 = s0
    q_give = og.at[0]
    t0n, t0f = tn, tf
    r1n = x0.at[pl.ds(pair, rows)]
    r0n = x0.at[pl.ds(pair + rows, cut)]
    r0f = x0.at[pl.ds(pair + rows + cut, cut)]

    r = lax.axis_index("replica")
    t = lax.axis_index("tensor")
    lower = (r // 2) % 2
    keep0 = lower * half
    give0 = (1 - lower) * half
    r_near = r + 1 - 2 * (r % 2)
    t_core = t + 1 - 2 * (t % 2)
    t_far = (t + 2) % 4
    core = (r, t_core)
    near = (r_near, t)
    far = (r_near, t_far)
    across = (r + 2 - 4 * lower, t)
    beyond = (r, t_far)

    barrier = pltpu.get_barrier_semaphore()
    for there in (core, near, far, across, beyond):
        pl.semaphore_signal(barrier, inc=1, device_id=there, device_id_type=pl.DeviceIdType.MESH)
    pl.semaphore_wait(barrier, 5)

    def piece(start, size):
        return pl.ds(pl.multiple_of(start, size), size)

    def remote(k, src, dst, there):
        return pltpu.make_async_remote_copy(
            src_ref=src, dst_ref=dst, send_sem=send.at[k], recv_sem=recv.at[k],
            device_id=there, device_id_type=pl.DeviceIdType.MESH,
        )

    routes = {
        "x0n0": (x_hbm.at[0, pl.ds(cut, piece_rows)], tn.at[pl.ds(0, piece_rows)], near),
        "x0n1": (x_hbm.at[0, pl.ds(most, piece_rows)], tn.at[pl.ds(piece_rows, piece_rows)], near),
        "x0f0": (x_hbm.at[0, pl.ds(0, piece_rows)], tf.at[pl.ds(0, piece_rows)], far),
        "x0f1": (x_hbm.at[0, pl.ds(piece_rows, piece_rows)], tf.at[pl.ds(piece_rows, piece_rows)], far),
        "x0c0": (x_hbm.at[0], x0.at[pl.ds(pair, rows)], core),
        "x0fn0": (tf.at[pl.ds(0, piece_rows)], x0.at[pl.ds(rows, piece_rows)], near),
        "x0fn1": (tf.at[pl.ds(piece_rows, piece_rows)], x0.at[pl.ds(rows + piece_rows, piece_rows)], near),
        "x0nf0": (tn.at[pl.ds(0, piece_rows)], x0.at[pl.ds(rows + cut, piece_rows)], far),
        "x0nf1": (tn.at[pl.ds(piece_rows, piece_rows)], x0.at[pl.ds(rows + most, piece_rows)], far),
        "x0c1": (x0.at[pl.ds(rows, rows)], x0.at[pl.ds(pair + rows, rows)], core),
        "x1n0": (x_hbm.at[1, pl.ds(0, cut)], xb.at[pl.ds(0, cut)], near),
        "x1n1": (x_hbm.at[1, pl.ds(cut, cut)], xb.at[pl.ds(cut, cut)], near),
        "x1f": (x_hbm.at[1], xb.at[pl.ds(rows, rows)], far),
        "x1c": (x_hbm.at[1], xa.at[pl.ds(pair, rows)], core),
        "x1nf0": (xb.at[pl.ds(0, cut)], xa.at[pl.ds(rows, cut)], far),
        "x1nf1": (xb.at[pl.ds(cut, cut)], xa.at[pl.ds(rows + cut, cut)], far),
        "x1c1": (xa.at[pl.ds(rows, rows)], xa.at[pl.ds(pair + rows, rows)], core),
        "xbc": (xb.at[pl.ds(0, pair)], xb.at[pl.ds(pair, pair)], core),
        "xca": (x_hbm.at[1], xc.at[pl.ds(0, rows)], across),
        "xcb": (xa.at[pl.ds(rows, piece_rows)], xc.at[pl.ds(rows, piece_rows)], across),
        "xcd": (xc.at[pl.ds(piece_rows, most)], xc.at[pl.ds(rows + piece_rows, most)], beyond),
        "xcc": (xc.at[pl.ds(0, pair)], xc.at[pl.ds(pair, pair)], core),
        "q": (q_give, q_got, near),
        "s1n": (s1, s1b, near),
        "s1x": (s1, s1c, across),
        "s1c": (s1.at[pl.ds(pair, pair)], s1o, core),
        "s1bc": (s1b.at[pl.ds(pair, pair)], s1bo, core),
        "st": (stepped, stepped_o, core),
        "p0c": (x0.at[pl.ds(pair, pair)], lp0, core),
        "a0f": (lp0.at[pl.ds(rows, cut)], t0f, far),
        "a0n": (lp0.at[pl.ds(rows + cut, cut)], t0n, near),
        "a0fn": (t0f, r0n, near),
        "a0nf": (t0n, r0f, far),
        "a1f": (xb.at[pl.ds(rows, rows)], t1f, far),
        "to_near": (xb.at[pl.ds(pair, rows)], r1n, near),
        "to_far": (xb.at[pl.ds(pair + rows, rows)], r1f, far),
    }

    def copy(name):
        return remote(NUMBER[name], *routes[name])

    def go(*names):
        for name in names:
            copy(name).start()

    def arrived(*names):
        for name in names:
            copy(name).wait_recv()

    def sent(*names):
        for name in names:
            copy(name).wait_send()

    def link(name, i):
        here = piece(i * chunk, chunk)
        give = piece(give0 + i * chunk, chunk)
        src, dst, there = {
            "w1": (w_hbm.at[0, give], lw1.at[here], across),
            "w2": (lw1.at[here], lw2.at[here], near),
            "w3": (lw2.at[here], lw3.at[here], across),
            "m1": (mv.at[give], lm1.at[here], across),
            "m2": (lm1.at[here], lm2.at[here], near),
            "m3": (lm2.at[here], lm3.at[here], across),
        }[name]
        return remote(CHAINS[name] + i, src, dst, there)

    def load(k, src, dst):
        return pltpu.make_async_copy(src, dst, local.at[k])

    loads = [
        load(0, x_hbm.at[0], x0.at[pl.ds(0, rows)]),
        load(1, w_hbm.at[0], wv),
        load(2, og_hbm, og),
        load(3, x_hbm.at[1], xa.at[pl.ds(0, rows)]),
        load(4, m_hbm.at[0], mv),
    ]

    def each(count, body):
        @pl.loop(0, count)
        def _(i):
            body(i)

    loads[0].start()
    go("x0f0", "x0n0", "x0f1", "x0n1", "x0c0")
    each(CHUNKS, lambda i: link("w1", i).start())
    for load_now in loads[1:]:
        load_now.start()
    for k in "01":
        arrived("x0f" + k)
        go("x0fn" + k)
        arrived("x0n" + k)
        go("x0nf" + k)
    go("x1n0", "x1n1", "x1f", "x1c")
    loads[1].wait()

    def pair_chunk(own, landed, first, second, i):
        link(first, i).wait_recv()
        here = piece(i * chunk, chunk)
        mine = own[piece(keep0 + i * chunk, chunk), :].astype(f32)
        landed[here, :] = ((mine + landed[here, :].astype(f32)) * 0.5).astype(bf16)
        link(second, i).start()

    def mean_chunk(landed, other, second, third, i):
        link(second, i).wait_recv()
        here = piece(i * chunk, chunk)
        other[here, :] = ((landed[here, :].astype(f32) + other[here, :].astype(f32)) * 0.5).astype(bf16)
        link(third, i).start()

    def w_pairs(first, last):
        each(last - first, lambda i: pair_chunk(wv, lw1, "w1", "w2", i + first))

    def m_pairs(first, last):
        each(last - first, lambda i: pair_chunk(mv, lm1, "m1", "m2", i + first))

    w_pairs(0, 2)
    loads[0].wait()
    loads[2].wait()
    arrived("x0c0", "x0fn0", "x0fn1", "x0nf0", "x0nf1")
    go("x0c1")
    arrived("x0c1")

    depth = d // 8

    def product(out, lhs, rhs):
        out[...] = jnp.zeros_like(out)

        def add(k):
            here = piece(k * depth, depth)
            out[...] += dot(lhs[:, here], rhs[here, :], 1, 0)

        each(d // depth, add)

    def slopes(out, step, pre):
        for j, block in enumerate((t, t_far, t_core, (t_core + 2) % 4)):
            up = og[step, piece(block * rows, rows), :].astype(f32)
            here = pl.ds(j * rows, rows)
            out[here, :] = (up * silu_slope(pre(here))).astype(bf16)

    product(q_own, x0, wv)
    slopes(s0, 0, lambda here: q_own[here, :])
    loads[4].wait()

    def moment_tile(start):
        here = piece(start, chunk)
        grad = dot(x0[:, here], s0[...], 0, 0)
        moment = (mom_decay * mv[here, :].astype(f32) + grad).astype(bf16)
        mv[here, :] = moment
        stepped[here, :] = (wv[here, :].astype(f32) - learn_rate * moment.astype(f32)).astype(bf16)

    def moment_chunk(i):
        moment_tile(give0 + i * chunk)
        link("m1", i).start()

    each(CHUNKS, moment_chunk)
    each(CHUNKS, lambda i: moment_tile(keep0 + i * chunk))
    go("st", "xca")

    sent("x0c1")
    arrived("x1n0")
    go("x1nf0")

    def part0(first):
        def one(k):
            here = piece(k * chunk, chunk)
            x0[pl.ds(first, pair), here] = dot(s0[pl.ds(first, pair), :], wv[here, :], 1, 1).astype(bf16)

        each(d // chunk, one)

    part0(pair)
    go("p0c")
    part0(0)

    arrived("x1n1")
    sent("x0fn0", "x0fn1", "x0nf0", "x0nf1")
    go("x1nf1")
    arrived("x1f")
    go("xbc")
    arrived("p0c")
    lp0[pl.ds(rows, rows), :] = (
        x0[pl.ds(rows, rows), :].astype(f32) + lp0[pl.ds(rows, rows), :].astype(f32)
    ).astype(bf16)

    w_pairs(2, 3)
    arrived("xbc")
    product(q_own, xb, stepped)
    q_give[...] = q_own[...].astype(bf16)
    go("q")
    w_pairs(3, 6)
    loads[3].wait()
    arrived("x1nf0", "x1nf1")
    go("x1c1", "xcb")
    arrived("x1c", "x1c1")
    product(q_own, xa, stepped)
    arrived("q")
    sent("p0c")
    slopes(s1, 1, lambda here: (q_own[here, :] + q_got[here, :].astype(f32)) * 0.5)
    go("s1n", "s1x", "s1c")
    w_pairs(6, CHUNKS)
    m_pairs(0, CHUNKS // 2)
    arrived("s1n")
    go("s1bc")
    arrived("s1c", "s1bc", "st")

    sent("x1nf0", "x1nf1", "xbc")

    def part1(k):
        here = piece(k * chunk, chunk)
        mine = jnp.concatenate([s1[pl.ds(0, pair), :], s1b[pl.ds(0, pair), :]], axis=0)
        theirs = jnp.concatenate([s1o[...], s1bo[...]], axis=0)
        both = dot(mine, stepped[here, :], 1, 1) + dot(theirs, stepped_o[here, :], 1, 1)
        xb[:, here] = (both * 0.5).astype(bf16)

    each(d // chunk, part1)
    go("a1f", "to_far")

    m_pairs(CHUNKS // 2, CHUNKS)
    each(CHUNKS, lambda i: mean_chunk(lw1, lw2, "w2", "w3", i))
    arrived("xca")
    go("xcd", "a0n", "a0f")
    arrived("a1f")
    here = pl.ds(pair, rows)
    xb[here, :] = (xb[here, :].astype(f32) + t1f[...].astype(f32)).astype(bf16)
    go("to_near")
    each(CHUNKS, lambda i: mean_chunk(lm1, lm2, "m2", "m3", i))
    arrived("a0f")
    go("a0fn")
    arrived("xcb", "xcd")
    go("xcc")
    arrived("a0n")
    go("a0nf")

    arrived("s1x", "xcc")
    each(CHUNKS, lambda i: link("m1", i).wait_send())

    def finish(w_mean, m_mean, start, i, wait):
        from_ = piece(i * chunk, chunk)
        here = piece(start + i * chunk, chunk)
        if wait:
            link("w3", i).wait_recv()
            link("m3", i).wait_recv()
        grad = dot(xa[:, here], s1[...], 0, 0) + dot(xc[:, here], s1c[...], 0, 0)
        m_now = m_mean[from_, :].astype(f32)
        moment = (mom_decay * m_now + grad * 0.5).astype(bf16)
        mv[here, :] = moment
        wv[here, :] = (
            w_mean[from_, :].astype(f32) - learn_rate * (m_now + moment.astype(f32))
        ).astype(bf16)

    each(CHUNKS, lambda i: finish(lw2, lm2, keep0, i, False))

    def finish_chunk(i):
        finish(lw3, lm3, give0, i, True)

    each(CHUNKS - 1, finish_chunk)

    arrived("a0fn", "a0nf")
    for k, back in enumerate((r0n, r0f)):
        here = pl.ds(k * cut, cut)
        grad_in[0, here, :] = (
            x0[here, :].astype(f32) + lp0[here, :].astype(f32) + back[...].astype(f32)
        ).astype(bf16)
    arrived("to_near", "to_far")
    x_first = xb[pl.ds(0, rows), :].astype(f32)
    grad_in[1, :, :] = (x_first + r1n[...].astype(f32) + r1f[...].astype(f32)).astype(bf16)
    finish_chunk(CHUNKS - 1)

    sent(*[name for name in TRANSFERS if name not in AWAITED])

    def drain(i):
        for name in ("w1", "w2", "w3", "m2", "m3"):
            link(name, i).wait_send()

    each(CHUNKS, drain)


def write_out(w_in, m_in, g_in, w_out, m_out, g_out, done):
    copies = [
        pltpu.make_async_copy(src, dst, done.at[k])
        for k, (src, dst) in enumerate(((w_in, w_out), (m_in, m_out), (g_in, g_out)))
    ]
    for c in copies:
        c.start()
    for c in copies:
        c.wait()


def local(weight, momentum, inputs, out_grads):
    d, cols = weight.shape[1:]
    rows = inputs.shape[1]
    n, pair, cut, half = 4 * rows, 2 * rows, rows // 2, d // 2
    full = (d, cols)
    vmem = (
        [(full, bf16)] * 2
        + [((n, d), bf16)] * 4
        + [((half, cols), bf16)] * 6
        + [((cut, d), bf16)] * 2
        + [((pair, d), bf16)]
        + [((rows, d), bf16)] * 2
        + [((n, cols), f32)]
        + [((n, cols), bf16)]
        + [((2, n, cols), bf16)]
        + [((n, cols), bf16)] * 3
        + [((pair, cols), bf16)] * 2
    )
    results = pl.pallas_call(
        kernel,
        out_shape=(
            pltpu.VMEM(weight.shape, bf16),
            pltpu.VMEM(momentum.shape, bf16),
            pltpu.VMEM(inputs.shape, bf16),
        ),
        in_specs=[pl.BlockSpec(memory_space=pl.ANY)] * 4,
        out_specs=[pl.BlockSpec(memory_space=pltpu.VMEM)] * 3,
        scratch_shapes=[pltpu.VMEM(shape, kind) for shape, kind in vmem]
        + [
            pltpu.SemaphoreType.DMA((COPIES,)),
            pltpu.SemaphoreType.DMA((COPIES,)),
            pltpu.SemaphoreType.DMA((5,)),
        ],
        compiler_params=pltpu.CompilerParams(
            collective_id=0, has_side_effects=True, vmem_limit_bytes=53 << 20
        ),
    )(weight, momentum, inputs, out_grads)
    return pl.pallas_call(
        write_out,
        out_shape=[jax.ShapeDtypeStruct(a.shape, bf16) for a in (weight, momentum, inputs)],
        in_specs=[pl.BlockSpec(memory_space=pltpu.VMEM)] * 3,
        out_specs=[pl.BlockSpec(memory_space=pl.ANY)] * 3,
        scratch_shapes=[pltpu.SemaphoreType.DMA((3,))],
        compiler_params=pltpu.CompilerParams(vmem_limit_bytes=1 << 20),
    )(*results)


def solution(mesh):
    return jax.shard_map(
        local,
        mesh=mesh,
        in_specs=(
            P("replica", None, "tensor"),
            P("replica", None, "tensor"),
            P(None, ("replica", "tensor"), None),
            P(None, "replica", "tensor"),
        ),
        out_specs=(
            P("replica", None, "tensor"),
            P("replica", None, "tensor"),
            P(None, ("replica", "tensor"), None),
        ),
        check_vma=False,
    )
```

```python
import jax
import jax.numpy as jnp
from jax import lax
from jax.experimental import pallas as pl
from jax.experimental.pallas import tpu as pltpu
from jax.sharding import PartitionSpec as P

learn_rate = 0.001
mom_decay = 0.9

bf16 = jnp.bfloat16
f32 = jnp.float32

CHUNKS = 8
TRANSFERS = (
    "x0n0", "x0n1", "x0f0", "x0f1", "x0c0", "x0fn0", "x0fn1", "x0nf0", "x0nf1", "x0c1", "x1n0",
    "x1n1", "x1f", "x1c", "x1nf0", "x1nf1", "x1c1", "xbc", "xca", "xcb", "xcd", "xcc", "q", "s1n",
    "s1x", "s1c", "s1bc", "st", "p0c", "a0f", "a0n", "a0fn", "a0nf", "a1f", "to_near", "to_far",
)
NUMBER = {name: k for k, name in enumerate(TRANSFERS)}
AWAITED = ("x0c1", "x1nf0", "x1nf1", "xbc", "x0fn0", "x0fn1", "x0nf0", "x0nf1", "p0c")
CHAINS = {name: len(TRANSFERS) + CHUNKS * k for k, name in enumerate(("w1", "w2", "w3", "m1", "m2", "m3"))}
COPIES = len(TRANSFERS) + CHUNKS * len(CHAINS)


def silu_slope(pre):
    sigma = jax.nn.sigmoid(pre)
    return sigma * (1.0 + pre * (1.0 - sigma))


def dot(a, b, left, right):
    return lax.dot_general(a, b, (((left,), (right,)), ((), ())), preferred_element_type=f32)


def kernel(
    w_hbm, m_hbm, x_hbm, og_hbm, new_w, new_m, grad_in,
    stepped, stepped_o, x0, xa, xb, xc, lw1, lw2, lw3, lm1, lm2, lm3,
    tn, tf, lp0, t1f, r1f, q_own, q_got, og, s0, s1b, s1c, s1o, s1bo,
    send, recv, local,
):
    wv, mv = new_w.at[0], new_m.at[0]
    d, cols = stepped.shape
    rows = x0.shape[0] // 4
    cut = rows // 2
    half = d // 2
    chunk = half // CHUNKS
    piece_rows = cut // 2
    most = rows - cut // 2
    pair = 2 * rows
    s1 = s0
    q_give = og.at[0]
    t0n, t0f = tn, tf
    r1n = x0.at[pl.ds(pair, rows)]
    r0n = x0.at[pl.ds(pair + rows, cut)]
    r0f = x0.at[pl.ds(pair + rows + cut, cut)]

    r = lax.axis_index("replica")
    t = lax.axis_index("tensor")
    lower = (r // 2) % 2
    keep0 = lower * half
    give0 = (1 - lower) * half
    r_near = r + 1 - 2 * (r % 2)
    t_core = t + 1 - 2 * (t % 2)
    t_far = (t + 2) % 4
    core = (r, t_core)
    near = (r_near, t)
    far = (r_near, t_far)
    across = (r + 2 - 4 * lower, t)
    beyond = (r, t_far)

    barrier = pltpu.get_barrier_semaphore()
    for there in (core, near, far, across, beyond):
        pl.semaphore_signal(barrier, inc=1, device_id=there, device_id_type=pl.DeviceIdType.MESH)
    pl.semaphore_wait(barrier, 5)

    def piece(start, size):
        return pl.ds(pl.multiple_of(start, size), size)

    def remote(k, src, dst, there):
        return pltpu.make_async_remote_copy(
            src_ref=src, dst_ref=dst, send_sem=send.at[k], recv_sem=recv.at[k],
            device_id=there, device_id_type=pl.DeviceIdType.MESH,
        )

    routes = {
        "x0n0": (x_hbm.at[0, pl.ds(cut, piece_rows)], tn.at[pl.ds(0, piece_rows)], near),
        "x0n1": (x_hbm.at[0, pl.ds(most, piece_rows)], tn.at[pl.ds(piece_rows, piece_rows)], near),
        "x0f0": (x_hbm.at[0, pl.ds(0, piece_rows)], tf.at[pl.ds(0, piece_rows)], far),
        "x0f1": (x_hbm.at[0, pl.ds(piece_rows, piece_rows)], tf.at[pl.ds(piece_rows, piece_rows)], far),
        "x0c0": (x_hbm.at[0], x0.at[pl.ds(pair, rows)], core),
        "x0fn0": (tf.at[pl.ds(0, piece_rows)], x0.at[pl.ds(rows, piece_rows)], near),
        "x0fn1": (tf.at[pl.ds(piece_rows, piece_rows)], x0.at[pl.ds(rows + piece_rows, piece_rows)], near),
        "x0nf0": (tn.at[pl.ds(0, piece_rows)], x0.at[pl.ds(rows + cut, piece_rows)], far),
        "x0nf1": (tn.at[pl.ds(piece_rows, piece_rows)], x0.at[pl.ds(rows + most, piece_rows)], far),
        "x0c1": (x0.at[pl.ds(rows, rows)], x0.at[pl.ds(pair + rows, rows)], core),
        "x1n0": (x_hbm.at[1, pl.ds(0, cut)], xb.at[pl.ds(0, cut)], near),
        "x1n1": (x_hbm.at[1, pl.ds(cut, cut)], xb.at[pl.ds(cut, cut)], near),
        "x1f": (x_hbm.at[1], xb.at[pl.ds(rows, rows)], far),
        "x1c": (x_hbm.at[1], xa.at[pl.ds(pair, rows)], core),
        "x1nf0": (xb.at[pl.ds(0, cut)], xa.at[pl.ds(rows, cut)], far),
        "x1nf1": (xb.at[pl.ds(cut, cut)], xa.at[pl.ds(rows + cut, cut)], far),
        "x1c1": (xa.at[pl.ds(rows, rows)], xa.at[pl.ds(pair + rows, rows)], core),
        "xbc": (xb.at[pl.ds(0, pair)], xb.at[pl.ds(pair, pair)], core),
        "xca": (x_hbm.at[1], xc.at[pl.ds(0, rows)], across),
        "xcb": (xa.at[pl.ds(rows, piece_rows)], xc.at[pl.ds(rows, piece_rows)], across),
        "xcd": (xc.at[pl.ds(piece_rows, most)], xc.at[pl.ds(rows + piece_rows, most)], beyond),
        "xcc": (xc.at[pl.ds(0, pair)], xc.at[pl.ds(pair, pair)], core),
        "q": (q_give, q_got, near),
        "s1n": (s1, s1b, near),
        "s1x": (s1, s1c, across),
        "s1c": (s1.at[pl.ds(pair, pair)], s1o, core),
        "s1bc": (s1b.at[pl.ds(pair, pair)], s1bo, core),
        "st": (stepped, stepped_o, core),
        "p0c": (x0.at[pl.ds(pair, pair)], lp0, core),
        "a0f": (lp0.at[pl.ds(rows, cut)], t0f, far),
        "a0n": (lp0.at[pl.ds(rows + cut, cut)], t0n, near),
        "a0fn": (t0f, r0n, near),
        "a0nf": (t0n, r0f, far),
        "a1f": (xb.at[pl.ds(rows, rows)], t1f, far),
        "to_near": (xb.at[pl.ds(pair, rows)], r1n, near),
        "to_far": (xb.at[pl.ds(pair + rows, rows)], r1f, far),
    }

    def copy(name):
        return remote(NUMBER[name], *routes[name])

    def go(*names):
        for name in names:
            copy(name).start()

    def arrived(*names):
        for name in names:
            copy(name).wait_recv()

    def sent(*names):
        for name in names:
            copy(name).wait_send()

    def link(name, i):
        here = piece(i * chunk, chunk)
        give = piece(give0 + i * chunk, chunk)
        src, dst, there = {
            "w1": (w_hbm.at[0, give], lw1.at[here], across),
            "w2": (lw1.at[here], lw2.at[here], near),
            "w3": (lw2.at[here], lw3.at[here], across),
            "m1": (mv.at[give], lm1.at[here], across),
            "m2": (lm1.at[here], lm2.at[here], near),
            "m3": (lm2.at[here], lm3.at[here], across),
        }[name]
        return remote(CHAINS[name] + i, src, dst, there)

    def load(k, src, dst):
        return pltpu.make_async_copy(src, dst, local.at[k])

    loads = [
        load(0, x_hbm.at[0], x0.at[pl.ds(0, rows)]),
        load(1, w_hbm.at[0], wv),
        load(2, og_hbm, og),
        load(3, x_hbm.at[1], xa.at[pl.ds(0, rows)]),
        load(4, m_hbm.at[0], mv),
    ]

    def each(count, body):
        @pl.loop(0, count)
        def _(i):
            body(i)

    loads[0].start()
    go("x0f0", "x0n0", "x0f1", "x0n1", "x0c0")
    each(CHUNKS, lambda i: link("w1", i).start())
    for load_now in loads[1:]:
        load_now.start()
    for k in "01":
        arrived("x0f" + k)
        go("x0fn" + k)
        arrived("x0n" + k)
        go("x0nf" + k)
    go("x1n0", "x1n1", "x1f", "x1c")
    loads[1].wait()

    def pair_chunk(own, landed, first, second, i):
        link(first, i).wait_recv()
        here = piece(i * chunk, chunk)
        mine = own[piece(keep0 + i * chunk, chunk), :].astype(f32)
        landed[here, :] = ((mine + landed[here, :].astype(f32)) * 0.5).astype(bf16)
        link(second, i).start()

    def mean_chunk(landed, other, second, third, i):
        link(second, i).wait_recv()
        here = piece(i * chunk, chunk)
        other[here, :] = ((landed[here, :].astype(f32) + other[here, :].astype(f32)) * 0.5).astype(bf16)
        link(third, i).start()

    def w_pairs(first, last):
        each(last - first, lambda i: pair_chunk(wv, lw1, "w1", "w2", i + first))

    def m_pairs(first, last):
        each(last - first, lambda i: pair_chunk(mv, lm1, "m1", "m2", i + first))

    w_pairs(0, 2)
    loads[0].wait()
    loads[2].wait()
    arrived("x0c0", "x0fn0", "x0fn1", "x0nf0", "x0nf1")
    go("x0c1")
    arrived("x0c1")

    depth = d // 8

    def product(out, lhs, rhs):
        out[...] = jnp.zeros_like(out)

        def add(k):
            here = piece(k * depth, depth)
            out[...] += dot(lhs[:, here], rhs[here, :], 1, 0)

        each(d // depth, add)

    def slopes(out, step, pre):
        for j, block in enumerate((t, t_far, t_core, (t_core + 2) % 4)):
            up = og[step, piece(block * rows, rows), :].astype(f32)
            here = pl.ds(j * rows, rows)
            out[here, :] = (up * silu_slope(pre(here))).astype(bf16)

    product(q_own, x0, wv)
    slopes(s0, 0, lambda here: q_own[here, :])
    loads[4].wait()

    def moment_tile(start):
        here = piece(start, chunk)
        grad = dot(x0[:, here], s0[...], 0, 0)
        moment = (mom_decay * mv[here, :].astype(f32) + grad).astype(bf16)
        mv[here, :] = moment
        stepped[here, :] = (wv[here, :].astype(f32) - learn_rate * moment.astype(f32)).astype(bf16)

    def moment_chunk(i):
        moment_tile(give0 + i * chunk)
        link("m1", i).start()

    each(CHUNKS, moment_chunk)
    each(CHUNKS, lambda i: moment_tile(keep0 + i * chunk))
    go("st", "xca")

    sent("x0c1")
    arrived("x1n0")
    go("x1nf0")

    def part0(first):
        def one(k):
            here = piece(k * chunk, chunk)
            x0[pl.ds(first, pair), here] = dot(s0[pl.ds(first, pair), :], wv[here, :], 1, 1).astype(bf16)

        each(d // chunk, one)

    part0(pair)
    go("p0c")
    part0(0)

    arrived("x1n1")
    sent("x0fn0", "x0fn1", "x0nf0", "x0nf1")
    go("x1nf1")
    arrived("x1f")
    go("xbc")
    arrived("p0c")
    lp0[pl.ds(rows, rows), :] = (
        x0[pl.ds(rows, rows), :].astype(f32) + lp0[pl.ds(rows, rows), :].astype(f32)
    ).astype(bf16)

    w_pairs(2, 3)
    arrived("xbc")
    product(q_own, xb, stepped)
    q_give[...] = q_own[...].astype(bf16)
    go("q")
    w_pairs(3, 6)
    loads[3].wait()
    arrived("x1nf0", "x1nf1")
    go("x1c1", "xcb")
    arrived("x1c", "x1c1")
    product(q_own, xa, stepped)
    arrived("q")
    sent("p0c")
    slopes(s1, 1, lambda here: (q_own[here, :] + q_got[here, :].astype(f32)) * 0.5)
    go("s1n", "s1x", "s1c")
    w_pairs(6, CHUNKS)
    m_pairs(0, CHUNKS // 2)
    arrived("s1n")
    go("s1bc")
    arrived("s1c", "s1bc", "st")

    sent("x1nf0", "x1nf1", "xbc")

    def part1(k):
        here = piece(k * chunk, chunk)
        mine = jnp.concatenate([s1[pl.ds(0, pair), :], s1b[pl.ds(0, pair), :]], axis=0)
        theirs = jnp.concatenate([s1o[...], s1bo[...]], axis=0)
        both = dot(mine, stepped[here, :], 1, 1) + dot(theirs, stepped_o[here, :], 1, 1)
        xb[:, here] = (both * 0.5).astype(bf16)

    each(d // chunk, part1)
    go("a1f", "to_far")

    m_pairs(CHUNKS // 2, CHUNKS)
    each(CHUNKS, lambda i: mean_chunk(lw1, lw2, "w2", "w3", i))
    arrived("xca")
    go("xcd", "a0n", "a0f")
    arrived("a1f")
    here = pl.ds(pair, rows)
    xb[here, :] = (xb[here, :].astype(f32) + t1f[...].astype(f32)).astype(bf16)
    go("to_near")
    each(CHUNKS, lambda i: mean_chunk(lm1, lm2, "m2", "m3", i))
    arrived("a0f")
    go("a0fn")
    arrived("xcb", "xcd")
    go("xcc")
    arrived("a0n")
    go("a0nf")

    arrived("s1x", "xcc")
    each(CHUNKS, lambda i: link("m1", i).wait_send())

    def gradient(here):
        return dot(xa[:, here], s1[...], 0, 0) + dot(xc[:, here], s1c[...], 0, 0)

    def finish(w_mean, m_mean, from_, here, grad):
        m_now = m_mean[from_, :].astype(f32)
        moment = (mom_decay * m_now + grad * 0.5).astype(bf16)
        mv[here, :] = moment
        wv[here, :] = (
            w_mean[from_, :].astype(f32) - learn_rate * (m_now + moment.astype(f32))
        ).astype(bf16)

    def finish_kept(i):
        here = piece(keep0 + i * chunk, chunk)
        finish(lw2, lm2, piece(i * chunk, chunk), here, gradient(here))

    def finish_chunk(i):
        here = piece(give0 + i * chunk, chunk)
        link("w3", i).wait_recv()
        link("m3", i).wait_recv()
        finish(lw3, lm3, piece(i * chunk, chunk), here, gradient(here))

    each(CHUNKS, finish_kept)
    each(CHUNKS - 2, finish_chunk)

    last = CHUNKS - 1
    here = piece(give0 + last * chunk, chunk)
    grad_last = q_own.at[pl.ds(0, chunk)]
    grad_last[...] = gradient(here)

    def drain(i):
        for name in ("w1", "w2", "w3", "m2"):
            link(name, i).wait_send()

    late = ("to_near", "to_far", "a0fn", "a0nf")
    each(CHUNKS, drain)
    sent(*[name for name in TRANSFERS if name not in AWAITED + late])
    arrived("to_near", "to_far")
    x_first = xb[pl.ds(0, rows), :].astype(f32)
    grad_in[1, :, :] = (x_first + r1n[...].astype(f32) + r1f[...].astype(f32)).astype(bf16)
    finish_chunk(last - 1)
    each(last, lambda i: link("m3", i).wait_send())
    arrived("a0fn", "a0nf")
    for k, back in enumerate((r0n, r0f)):
        rows_of = pl.ds(k * cut, cut)
        grad_in[0, rows_of, :] = (
            x0[rows_of, :].astype(f32) + lp0[rows_of, :].astype(f32) + back[...].astype(f32)
        ).astype(bf16)
    sent(*late)
    link("w3", last).wait_recv()
    link("m3", last).wait_recv()
    finish(lw3, lm3, piece(last * chunk, chunk), here, grad_last[...])
    link("m3", last).wait_send()


def write_out(w_in, m_in, g_in, w_out, m_out, g_out, done):
    parts = 4
    size = w_in.shape[1] // parts
    pieces = [(g_in, g_out)]
    for k in range(parts):
        here = pl.ds(k * size, size)
        pieces += [(w_in.at[0, here], w_out.at[0, here]), (m_in.at[0, here], m_out.at[0, here])]
    copies = [
        pltpu.make_async_copy(src, dst, done.at[k]) for k, (src, dst) in enumerate(pieces)
    ]
    for c in copies:
        c.start()
    for c in copies:
        c.wait()


def local(weight, momentum, inputs, out_grads):
    d, cols = weight.shape[1:]
    rows = inputs.shape[1]
    n, pair, cut, half = 4 * rows, 2 * rows, rows // 2, d // 2
    full = (d, cols)
    vmem = (
        [(full, bf16)] * 2
        + [((n, d), bf16)] * 4
        + [((half, cols), bf16)] * 6
        + [((cut, d), bf16)] * 2
        + [((pair, d), bf16)]
        + [((rows, d), bf16)] * 2
        + [((n, cols), f32)]
        + [((n, cols), bf16)]
        + [((2, n, cols), bf16)]
        + [((n, cols), bf16)] * 3
        + [((pair, cols), bf16)] * 2
    )
    results = pl.pallas_call(
        kernel,
        out_shape=(
            pltpu.VMEM(weight.shape, bf16),
            pltpu.VMEM(momentum.shape, bf16),
            pltpu.VMEM(inputs.shape, bf16),
        ),
        in_specs=[pl.BlockSpec(memory_space=pl.ANY)] * 4,
        out_specs=[pl.BlockSpec(memory_space=pltpu.VMEM)] * 3,
        scratch_shapes=[pltpu.VMEM(shape, kind) for shape, kind in vmem]
        + [
            pltpu.SemaphoreType.DMA((COPIES,)),
            pltpu.SemaphoreType.DMA((COPIES,)),
            pltpu.SemaphoreType.DMA((5,)),
        ],
        compiler_params=pltpu.CompilerParams(
            collective_id=0, has_side_effects=True, vmem_limit_bytes=53 << 20
        ),
    )(weight, momentum, inputs, out_grads)
    return pl.pallas_call(
        write_out,
        out_shape=[jax.ShapeDtypeStruct(a.shape, bf16) for a in (weight, momentum, inputs)],
        in_specs=[pl.BlockSpec(memory_space=pltpu.VMEM)] * 3,
        out_specs=[pl.BlockSpec(memory_space=pl.ANY)] * 3,
        scratch_shapes=[pltpu.SemaphoreType.DMA((9,))],
        compiler_params=pltpu.CompilerParams(vmem_limit_bytes=1 << 20),
    )(*results)


def solution(mesh):
    return jax.shard_map(
        local,
        mesh=mesh,
        in_specs=(
            P("replica", None, "tensor"),
            P("replica", None, "tensor"),
            P(None, ("replica", "tensor"), None),
            P(None, "replica", "tensor"),
        ),
        out_specs=(
            P("replica", None, "tensor"),
            P("replica", None, "tensor"),
            P(None, ("replica", "tensor"), None),
        ),
        check_vma=False,
    )
```

```python
import jax
import jax.numpy as jnp
from jax import lax
from jax.experimental import pallas as pl
from jax.experimental.pallas import tpu as pltpu
from jax.sharding import PartitionSpec as P

learn_rate = 0.001
mom_decay = 0.9

bf16 = jnp.bfloat16
f32 = jnp.float32

CHUNKS = 8
TRANSFERS = (
    "x0n0", "x0n1", "x0f0", "x0f1", "x0c0", "x0fn0", "x0fn1", "x0nf0", "x0nf1", "x0c1", "x1n0",
    "x1n1", "x1f", "x1c", "x1nf0", "x1nf1", "x1c1", "xbc", "q", "s1n", "s1c", "s1bc", "st", "p0c",
    "a0f", "a0n", "a0fn", "a0nf", "a1f", "to_near", "to_far", "pg", "pk", "px", "pm",
)
NUMBER = {name: k for k, name in enumerate(TRANSFERS)}
AWAITED = ("x0c1", "x1nf0", "x1nf1", "xbc", "x0fn0", "x0fn1", "x0nf0", "x0nf1", "p0c", "pg", "pk")
CHAINS = {
    name: len(TRANSFERS) + CHUNKS * k
    for k, name in enumerate(("w1", "w2", "w3", "m1", "m2", "m3", "g"))
}
COPIES = len(TRANSFERS) + CHUNKS * len(CHAINS)


def silu_slope(pre):
    sigma = jax.nn.sigmoid(pre)
    return sigma * (1.0 + pre * (1.0 - sigma))


def dot(a, b, left, right):
    return lax.dot_general(a, b, (((left,), (right,)), ((), ())), preferred_element_type=f32)


def kernel(
    w_hbm, m_hbm, x_hbm, og_hbm, new_w, new_m, grad_in,
    stepped, stepped_o, x0, xa, xb, lw1, lw2, lw3, lm1, lm2, lm3,
    tn, tf, lp0, t1f, r1f, q_own, q_got, og, s0, s1b, s1o, s1bo,
    g_give, g_got, lpg, lpk, lpx,
    send, recv, local,
):
    wv, mv = new_w.at[0], new_m.at[0]
    d, cols = stepped.shape
    rows = x0.shape[0] // 4
    cut = rows // 2
    half = d // 2
    chunk = half // CHUNKS
    piece_rows = cut // 2
    most = rows - cut // 2
    pair = 2 * rows
    s1 = s0
    q_give = og.at[0]
    t0n, t0f = tn, tf
    r1n = x0.at[pl.ds(pair, rows)]
    r0n = x0.at[pl.ds(pair + rows, cut)]
    r0f = x0.at[pl.ds(pair + rows + cut, cut)]

    r = lax.axis_index("replica")
    t = lax.axis_index("tensor")
    lower = (r // 2) % 2
    keep0 = lower * half
    give0 = (1 - lower) * half
    r_near = r + 1 - 2 * (r % 2)
    t_core = t + 1 - 2 * (t % 2)
    t_far = (t + 2) % 4
    core = (r, t_core)
    near = (r_near, t)
    far = (r_near, t_far)
    across = (r + 2 - 4 * lower, t)
    direct = CHUNKS // 2
    block0 = direct * chunk
    sub = (half - block0) // 2
    mine0 = block0 + (r % 2) * sub
    theirs0 = block0 + (1 - r % 2) * sub

    barrier = pltpu.get_barrier_semaphore()
    for there in (core, near, far, across):
        pl.semaphore_signal(barrier, inc=1, device_id=there, device_id_type=pl.DeviceIdType.MESH)
    pl.semaphore_wait(barrier, 4)

    def piece(start, size):
        return pl.ds(pl.multiple_of(start, size), size)

    def remote(k, src, dst, there):
        return pltpu.make_async_remote_copy(
            src_ref=src, dst_ref=dst, send_sem=send.at[k], recv_sem=recv.at[k],
            device_id=there, device_id_type=pl.DeviceIdType.MESH,
        )

    routes = {
        "x0n0": (x_hbm.at[0, pl.ds(cut, piece_rows)], tn.at[pl.ds(0, piece_rows)], near),
        "x0n1": (x_hbm.at[0, pl.ds(most, piece_rows)], tn.at[pl.ds(piece_rows, piece_rows)], near),
        "x0f0": (x_hbm.at[0, pl.ds(0, piece_rows)], tf.at[pl.ds(0, piece_rows)], far),
        "x0f1": (x_hbm.at[0, pl.ds(piece_rows, piece_rows)], tf.at[pl.ds(piece_rows, piece_rows)], far),
        "x0c0": (x_hbm.at[0], x0.at[pl.ds(pair, rows)], core),
        "x0fn0": (tf.at[pl.ds(0, piece_rows)], x0.at[pl.ds(rows, piece_rows)], near),
        "x0fn1": (tf.at[pl.ds(piece_rows, piece_rows)], x0.at[pl.ds(rows + piece_rows, piece_rows)], near),
        "x0nf0": (tn.at[pl.ds(0, piece_rows)], x0.at[pl.ds(rows + cut, piece_rows)], far),
        "x0nf1": (tn.at[pl.ds(piece_rows, piece_rows)], x0.at[pl.ds(rows + most, piece_rows)], far),
        "x0c1": (x0.at[pl.ds(rows, rows)], x0.at[pl.ds(pair + rows, rows)], core),
        "x1n0": (x_hbm.at[1, pl.ds(0, cut)], xb.at[pl.ds(0, cut)], near),
        "x1n1": (x_hbm.at[1, pl.ds(cut, cut)], xb.at[pl.ds(cut, cut)], near),
        "x1f": (x_hbm.at[1], xb.at[pl.ds(rows, rows)], far),
        "x1c": (x_hbm.at[1], xa.at[pl.ds(pair, rows)], core),
        "x1nf0": (xb.at[pl.ds(0, cut)], xa.at[pl.ds(rows, cut)], far),
        "x1nf1": (xb.at[pl.ds(cut, cut)], xa.at[pl.ds(rows + cut, cut)], far),
        "x1c1": (xa.at[pl.ds(rows, rows)], xa.at[pl.ds(pair + rows, rows)], core),
        "xbc": (xb.at[pl.ds(0, pair)], xb.at[pl.ds(pair, pair)], core),
        "q": (q_give, q_got, near),
        "s1n": (s1, s1b, near),
        "s1c": (s1.at[pl.ds(pair, pair)], s1o, core),
        "s1bc": (s1b.at[pl.ds(pair, pair)], s1bo, core),
        "st": (stepped, stepped_o, core),
        "p0c": (x0.at[pl.ds(pair, pair)], lp0, core),
        "a0f": (lp0.at[pl.ds(rows, cut)], t0f, far),
        "a0n": (lp0.at[pl.ds(rows + cut, cut)], t0n, near),
        "a0fn": (t0f, r0n, near),
        "a0nf": (t0n, r0f, far),
        "a1f": (xb.at[pl.ds(rows, rows)], t1f, far),
        "to_near": (xb.at[pl.ds(pair, rows)], r1n, near),
        "to_far": (xb.at[pl.ds(pair + rows, rows)], r1f, far),
        "pg": (mv.at[piece(give0 + theirs0, sub)], lpg, near),
        "pk": (mv.at[piece(keep0 + theirs0, sub)], lpk, near),
        "px": (lpg, lpx, across),
        "pm": (lm2.at[piece(mine0, sub)], lm2.at[piece(mine0, sub)], near),
    }

    def copy(name):
        return remote(NUMBER[name], *routes[name])

    def go(*names):
        for name in names:
            copy(name).start()

    def arrived(*names):
        for name in names:
            copy(name).wait_recv()

    def sent(*names):
        for name in names:
            copy(name).wait_send()

    def link(name, i):
        here = piece(i * chunk, chunk)
        give = piece(give0 + i * chunk, chunk)
        src, dst, there = {
            "w1": (w_hbm.at[0, give], lw1.at[here], across),
            "w2": (lw1.at[here], lw2.at[here], near),
            "w3": (lw2.at[here], lw3.at[here], across),
            "m1": (mv.at[give], lm1.at[here], across),
            "m2": (lm1.at[here], lm2.at[here], near),
            "m3": (mv.at[piece(keep0 + i * chunk, chunk)], lm3.at[here], across),
            "g": (g_give.at[here], g_got.at[here], across),
        }[name]
        return remote(CHAINS[name] + i, src, dst, there)

    def load(k, src, dst):
        return pltpu.make_async_copy(src, dst, local.at[k])

    loads = [
        load(0, x_hbm.at[0], x0.at[pl.ds(0, rows)]),
        load(1, w_hbm.at[0], wv),
        load(2, og_hbm, og),
        load(3, x_hbm.at[1], xa.at[pl.ds(0, rows)]),
        load(4, m_hbm.at[0], mv),
    ]

    def each(count, body):
        @pl.loop(0, count)
        def _(i):
            body(i)

    loads[0].start()
    go("x0f0", "x0n0", "x0f1", "x0n1", "x0c0")
    each(CHUNKS, lambda i: link("w1", i).start())
    for load_now in loads[1:]:
        load_now.start()
    for k in "01":
        arrived("x0f" + k)
        go("x0fn" + k)
        arrived("x0n" + k)
        go("x0nf" + k)
    go("x1n0", "x1n1", "x1f", "x1c")
    loads[1].wait()

    def pair_chunk(own, landed, first, second, i):
        link(first, i).wait_recv()
        here = piece(i * chunk, chunk)
        mine = own[piece(keep0 + i * chunk, chunk), :].astype(f32)
        landed[here, :] = ((mine + landed[here, :].astype(f32)) * 0.5).astype(bf16)
        link(second, i).start()

    def mean(out, left, right):
        out[...] = ((left[...].astype(f32) + right[...].astype(f32)) * 0.5).astype(bf16)

    def w_pairs(first, last):
        each(last - first, lambda i: pair_chunk(wv, lw1, "w1", "w2", i + first))

    def m_pairs(first, last):
        each(last - first, lambda i: pair_chunk(mv, lm1, "m1", "m2", i + first))

    loads[0].wait()
    loads[2].wait()
    arrived("x0c0", "x0fn0", "x0fn1", "x0nf0", "x0nf1")
    go("x0c1")
    arrived("x0c1")

    depth = d // 8

    def product(out, lhs, rhs):
        out[...] = jnp.zeros_like(out)

        def add(k):
            here = piece(k * depth, depth)
            out[...] += dot(lhs[:, here], rhs[here, :], 1, 0)

        each(d // depth, add)

    def slopes(out, step, pre):
        for j, block in enumerate((t, t_far, t_core, (t_core + 2) % 4)):
            up = og[step, piece(block * rows, rows), :].astype(f32)
            here = pl.ds(j * rows, rows)
            out[here, :] = (up * silu_slope(pre(here))).astype(bf16)

    product(q_own, x0, wv)
    slopes(s0, 0, lambda here: q_own[here, :])
    loads[4].wait()

    def moment_tile(start):
        here = piece(start, chunk)
        grad = dot(x0[:, here], s0[...], 0, 0)
        moment = (mom_decay * mv[here, :].astype(f32) + grad).astype(bf16)
        mv[here, :] = moment
        stepped[here, :] = (wv[here, :].astype(f32) - learn_rate * moment.astype(f32)).astype(bf16)

    def moment_chunk(i):
        moment_tile(give0 + i * chunk)
        link("m1", i).start()

    each(direct, moment_chunk)
    each(CHUNKS - direct, lambda i: moment_tile(give0 + (i + direct) * chunk))
    go("pg")
    w_pairs(0, 1)
    each(CHUNKS, lambda i: moment_tile(keep0 + i * chunk))
    go("st")

    sent("x0c1")
    arrived("x1n0")
    go("x1nf0")

    def part0(first):
        def one(k):
            here = piece(k * chunk, chunk)
            x0[pl.ds(first, pair), here] = dot(s0[pl.ds(first, pair), :], wv[here, :], 1, 1).astype(bf16)

        each(d // chunk, one)

    part0(pair)
    go("p0c")
    part0(0)

    arrived("x1n1")
    sent("x0fn0", "x0fn1", "x0nf0", "x0nf1")
    go("x1nf1")
    arrived("x1f")
    go("xbc")
    arrived("p0c")
    lp0[pl.ds(rows, rows), :] = (
        x0[pl.ds(rows, rows), :].astype(f32) + lp0[pl.ds(rows, rows), :].astype(f32)
    ).astype(bf16)

    arrived("xbc")
    product(q_own, xb, stepped)
    q_give[...] = q_own[...].astype(bf16)
    go("q")
    m_pairs(0, 1)
    w_pairs(1, 2)
    arrived("pg")
    mean(lpg, lpg, mv.at[piece(give0 + mine0, sub)])
    go("px")
    loads[3].wait()
    arrived("x1nf0", "x1nf1")
    go("x1c1")
    arrived("x1c", "x1c1")
    product(q_own, xa, stepped)
    arrived("q")
    sent("p0c")
    slopes(s1, 1, lambda here: (q_own[here, :] + q_got[here, :].astype(f32)) * 0.5)
    go("s1n", "s1c", "pk")

    def chunk_of(ref, i):
        return ref.at[piece(i * chunk, chunk)]

    def step_weights(i):
        w_mean = chunk_of(lw2, i)
        w_mean[...] = (
            w_mean[...].astype(f32) - learn_rate * chunk_of(lm2, i)[...].astype(f32)
        ).astype(bf16)
        link("w3", i).start()

    def direct_means(i):
        link("w2", i).wait_recv()
        mean(chunk_of(lw2, i), chunk_of(lw2, i), chunk_of(lw1, i))
        link("m2", i).wait_recv()
        mean(chunk_of(lm2, i), chunk_of(lm2, i), chunk_of(lm1, i))
        step_weights(i)

    def gradient(start):
        return dot(xa[:, piece(start, chunk)], s1[...], 0, 0) * 0.5

    def gradient_chunk(i):
        g_give[piece(i * chunk, chunk), :] = gradient(give0 + i * chunk).astype(bf16)
        link("g", i).start()

    direct_means(0)
    each(CHUNKS, gradient_chunk)
    w_pairs(2, 3)
    m_pairs(1, 2)
    w_pairs(3, 4)
    m_pairs(2, direct)
    w_pairs(4, CHUNKS)
    arrived("s1n")
    go("s1bc")
    arrived("s1c", "s1bc", "st")

    sent("x1nf0", "x1nf1", "xbc")

    def part1(k):
        here = piece(k * chunk, chunk)
        mine = jnp.concatenate([s1[pl.ds(0, pair), :], s1b[pl.ds(0, pair), :]], axis=0)
        theirs = jnp.concatenate([s1o[...], s1bo[...]], axis=0)
        both = dot(mine, stepped[here, :], 1, 1) + dot(theirs, stepped_o[here, :], 1, 1)
        xb[:, here] = (both * 0.5).astype(bf16)

    each(d // chunk, part1)
    go("a1f", "to_far")

    each(direct - 1, lambda i: direct_means(i + 1))
    arrived("pk", "px")
    mean(lpk, lpk, mv.at[piece(keep0 + mine0, sub)])
    mean(lm2.at[piece(mine0, sub)], lpk, lpx)
    go("pm")
    sent("pg", "pk")

    def finish_kept(i):
        link("g", i).wait_recv()
        here = piece(keep0 + i * chunk, chunk)
        grad = gradient(keep0 + i * chunk) + chunk_of(g_got, i)[...].astype(f32)
        moment = (mom_decay * chunk_of(lm2, i)[...].astype(f32) + grad).astype(bf16)
        mv[here, :] = moment
        link("m3", i).start()
        wv[here, :] = (
            chunk_of(lw2, i)[...].astype(f32) - learn_rate * moment.astype(f32)
        ).astype(bf16)

    arrived("a1f")
    here = pl.ds(pair, rows)
    xb[here, :] = (xb[here, :].astype(f32) + t1f[...].astype(f32)).astype(bf16)
    go("to_near", "a0n", "a0f")
    each(direct, finish_kept)

    arrived("pm")

    def later_weights(i):
        link("w2", i).wait_recv()
        mean(chunk_of(lw2, i), chunk_of(lw2, i), chunk_of(lw1, i))
        step_weights(i)

    each(CHUNKS - direct, lambda i: later_weights(i + direct))
    each(CHUNKS - direct, lambda i: finish_kept(i + direct))
    arrived("a0f")
    go("a0fn")
    each(direct, lambda i: link("m1", i).wait_send())

    def finish_given(i):
        link("w3", i).wait_recv()
        link("m3", i).wait_recv()
        here = piece(give0 + i * chunk, chunk)
        moment = chunk_of(lm3, i)[...]
        mv[here, :] = moment
        wv[here, :] = (
            chunk_of(lw3, i)[...].astype(f32) - learn_rate * moment.astype(f32)
        ).astype(bf16)

    each(direct, finish_given)
    arrived("a0n")
    go("a0nf")

    def drain(i):
        for name in ("w1", "w2", "w3", "g"):
            link(name, i).wait_send()

    late = ("to_near", "to_far", "a0fn", "a0nf")
    each(CHUNKS, drain)
    each(direct, lambda i: link("m2", i).wait_send())
    sent(*[name for name in TRANSFERS if name not in AWAITED + late])
    arrived("to_near", "to_far")
    x_first = xb[pl.ds(0, rows), :].astype(f32)
    grad_in[1, :, :] = (x_first + r1n[...].astype(f32) + r1f[...].astype(f32)).astype(bf16)
    last = CHUNKS - 1
    each(last - direct, lambda i: finish_given(i + direct))
    each(last, lambda i: link("m3", i).wait_send())
    arrived("a0fn", "a0nf")
    for k, back in enumerate((r0n, r0f)):
        rows_of = pl.ds(k * cut, cut)
        grad_in[0, rows_of, :] = (
            x0[rows_of, :].astype(f32) + lp0[rows_of, :].astype(f32) + back[...].astype(f32)
        ).astype(bf16)
    sent(*late)
    finish_given(last)
    link("m3", last).wait_send()


def write_out(w_in, m_in, g_in, w_out, m_out, g_out, done):
    parts = 4
    size = w_in.shape[1] // parts
    pieces = [(g_in, g_out)]
    for k in range(parts):
        here = pl.ds(k * size, size)
        pieces += [(w_in.at[0, here], w_out.at[0, here]), (m_in.at[0, here], m_out.at[0, here])]
    copies = [
        pltpu.make_async_copy(src, dst, done.at[k]) for k, (src, dst) in enumerate(pieces)
    ]
    for c in copies:
        c.start()
    for c in copies:
        c.wait()


def local(weight, momentum, inputs, out_grads):
    d, cols = weight.shape[1:]
    rows = inputs.shape[1]
    n, pair, cut, half = 4 * rows, 2 * rows, rows // 2, d // 2
    full = (d, cols)
    vmem = (
        [(full, bf16)] * 2
        + [((n, d), bf16)] * 3
        + [((half, cols), bf16)] * 6
        + [((cut, d), bf16)] * 2
        + [((pair, d), bf16)]
        + [((rows, d), bf16)] * 2
        + [((n, cols), f32)]
        + [((n, cols), bf16)]
        + [((2, n, cols), bf16)]
        + [((n, cols), bf16)] * 2
        + [((pair, cols), bf16)] * 2
        + [((half, cols), bf16)] * 2
        + [((half // 4, cols), bf16)] * 3
    )
    results = pl.pallas_call(
        kernel,
        out_shape=(
            pltpu.VMEM(weight.shape, bf16),
            pltpu.VMEM(momentum.shape, bf16),
            pltpu.VMEM(inputs.shape, bf16),
        ),
        in_specs=[pl.BlockSpec(memory_space=pl.ANY)] * 4,
        out_specs=[pl.BlockSpec(memory_space=pltpu.VMEM)] * 3,
        scratch_shapes=[pltpu.VMEM(shape, kind) for shape, kind in vmem]
        + [
            pltpu.SemaphoreType.DMA((COPIES,)),
            pltpu.SemaphoreType.DMA((COPIES,)),
            pltpu.SemaphoreType.DMA((5,)),
        ],
        compiler_params=pltpu.CompilerParams(
            collective_id=0, has_side_effects=True, vmem_limit_bytes=53 << 20
        ),
    )(weight, momentum, inputs, out_grads)
    return pl.pallas_call(
        write_out,
        out_shape=[jax.ShapeDtypeStruct(a.shape, bf16) for a in (weight, momentum, inputs)],
        in_specs=[pl.BlockSpec(memory_space=pltpu.VMEM)] * 3,
        out_specs=[pl.BlockSpec(memory_space=pl.ANY)] * 3,
        scratch_shapes=[pltpu.SemaphoreType.DMA((9,))],
        compiler_params=pltpu.CompilerParams(vmem_limit_bytes=1 << 20),
    )(*results)


def solution(mesh):
    return jax.shard_map(
        local,
        mesh=mesh,
        in_specs=(
            P("replica", None, "tensor"),
            P("replica", None, "tensor"),
            P(None, ("replica", "tensor"), None),
            P(None, "replica", "tensor"),
        ),
        out_specs=(
            P("replica", None, "tensor"),
            P("replica", None, "tensor"),
            P(None, ("replica", "tensor"), None),
        ),
        check_vma=False,
    )
```

```python
import jax
import jax.numpy as jnp
from jax import lax
from jax.experimental import pallas as pl
from jax.experimental.pallas import tpu as pltpu
from jax.sharding import PartitionSpec as P

learn_rate = 0.001
mom_decay = 0.9

bf16 = jnp.bfloat16
f32 = jnp.float32

CHUNKS = 8
TRANSFERS = (
    "x0n0", "x0n1", "x0f0", "x0f1", "x0c0", "x0fn0", "x0fn1", "x0nf0", "x0nf1", "x0c1", "x1n0",
    "x1n1", "x1f", "x1c", "x1nf0", "x1nf1", "x1c1", "xbc", "q", "s1n", "s1c", "s1bc", "st", "p0c",
    "a0f", "a0n", "a0fn", "a0nf", "a1f", "to_near", "to_far", "pg", "pk", "px", "pm",
)
NUMBER = {name: k for k, name in enumerate(TRANSFERS)}
AWAITED = ("x0c1", "x1nf0", "x1nf1", "xbc", "x0fn0", "x0fn1", "x0nf0", "x0nf1", "p0c", "pg", "pk")
CHAINS = {
    name: len(TRANSFERS) + CHUNKS * k
    for k, name in enumerate(("w1", "w2", "w3", "m1", "m2", "m3", "g"))
}
COPIES = len(TRANSFERS) + CHUNKS * len(CHAINS)


def silu_slope(pre):
    sigma = jax.nn.sigmoid(pre)
    return sigma * (1.0 + pre * (1.0 - sigma))


def dot(a, b, left, right):
    return lax.dot_general(a, b, (((left,), (right,)), ((), ())), preferred_element_type=f32)


def kernel(
    w_hbm, m_hbm, x_hbm, og_hbm, new_w, new_m, grad_in,
    stepped, stepped_o, x0, xa, xb, lw1, lw2, lw3, lm1, lm2, lm3,
    tn, tf, lp0, t1f, r1f, q_own, q_got, og, s0, s1b, s1o, s1bo,
    g_give, g_got, lpg, lpk, lpx,
    send, recv, local,
):
    wv, mv = new_w.at[0], new_m.at[0]
    d, cols = stepped.shape
    rows = x0.shape[0] // 4
    cut = rows // 2
    half = d // 2
    chunk = half // CHUNKS
    piece_rows = cut // 2
    most = rows - cut // 2
    pair = 2 * rows
    s1 = s0
    q_give = og.at[0]
    t0n, t0f = tn, tf
    r1n = x0.at[pl.ds(pair, rows)]
    r0n = x0.at[pl.ds(pair + rows, cut)]
    r0f = x0.at[pl.ds(pair + rows + cut, cut)]

    r = lax.axis_index("replica")
    t = lax.axis_index("tensor")
    lower = (r // 2) % 2
    keep0 = lower * half
    give0 = (1 - lower) * half
    r_near = r + 1 - 2 * (r % 2)
    t_core = t + 1 - 2 * (t % 2)
    t_far = (t + 2) % 4
    core = (r, t_core)
    near = (r_near, t)
    far = (r_near, t_far)
    across = (r + 2 - 4 * lower, t)
    direct = CHUNKS // 2
    block0 = direct * chunk
    sub = (half - block0) // 2
    mine0 = block0 + (r % 2) * sub
    theirs0 = block0 + (1 - r % 2) * sub

    barrier = pltpu.get_barrier_semaphore()
    for there in (core, near, far, across):
        pl.semaphore_signal(barrier, inc=1, device_id=there, device_id_type=pl.DeviceIdType.MESH)
    pl.semaphore_wait(barrier, 4)

    def piece(start, size):
        return pl.ds(pl.multiple_of(start, size), size)

    def remote(k, src, dst, there):
        return pltpu.make_async_remote_copy(
            src_ref=src, dst_ref=dst, send_sem=send.at[k], recv_sem=recv.at[k],
            device_id=there, device_id_type=pl.DeviceIdType.MESH,
        )

    routes = {
        "x0n0": (x_hbm.at[0, pl.ds(cut, piece_rows)], tn.at[pl.ds(0, piece_rows)], near),
        "x0n1": (x_hbm.at[0, pl.ds(most, piece_rows)], tn.at[pl.ds(piece_rows, piece_rows)], near),
        "x0f0": (x_hbm.at[0, pl.ds(0, piece_rows)], tf.at[pl.ds(0, piece_rows)], far),
        "x0f1": (x_hbm.at[0, pl.ds(piece_rows, piece_rows)], tf.at[pl.ds(piece_rows, piece_rows)], far),
        "x0c0": (x_hbm.at[0], x0.at[pl.ds(pair, rows)], core),
        "x0fn0": (tf.at[pl.ds(0, piece_rows)], x0.at[pl.ds(rows, piece_rows)], near),
        "x0fn1": (tf.at[pl.ds(piece_rows, piece_rows)], x0.at[pl.ds(rows + piece_rows, piece_rows)], near),
        "x0nf0": (tn.at[pl.ds(0, piece_rows)], x0.at[pl.ds(rows + cut, piece_rows)], far),
        "x0nf1": (tn.at[pl.ds(piece_rows, piece_rows)], x0.at[pl.ds(rows + most, piece_rows)], far),
        "x0c1": (x0.at[pl.ds(rows, rows)], x0.at[pl.ds(pair + rows, rows)], core),
        "x1n0": (x_hbm.at[1, pl.ds(0, cut)], xb.at[pl.ds(0, cut)], near),
        "x1n1": (x_hbm.at[1, pl.ds(cut, cut)], xb.at[pl.ds(cut, cut)], near),
        "x1f": (x_hbm.at[1], xb.at[pl.ds(rows, rows)], far),
        "x1c": (x_hbm.at[1], xa.at[pl.ds(pair, rows)], core),
        "x1nf0": (xb.at[pl.ds(0, cut)], xa.at[pl.ds(rows, cut)], far),
        "x1nf1": (xb.at[pl.ds(cut, cut)], xa.at[pl.ds(rows + cut, cut)], far),
        "x1c1": (xa.at[pl.ds(rows, rows)], xa.at[pl.ds(pair + rows, rows)], core),
        "xbc": (xb.at[pl.ds(0, pair)], xb.at[pl.ds(pair, pair)], core),
        "q": (q_give, q_got, near),
        "s1n": (s1, s1b, near),
        "s1c": (s1.at[pl.ds(pair, pair)], s1o, core),
        "s1bc": (s1b.at[pl.ds(pair, pair)], s1bo, core),
        "st": (stepped, stepped_o, core),
        "p0c": (x0.at[pl.ds(pair, pair)], lp0, core),
        "a0f": (lp0.at[pl.ds(rows, cut)], t0f, far),
        "a0n": (lp0.at[pl.ds(rows + cut, cut)], t0n, near),
        "a0fn": (t0f, r0n, near),
        "a0nf": (t0n, r0f, far),
        "a1f": (xb.at[pl.ds(rows, rows)], t1f, far),
        "to_near": (xb.at[pl.ds(pair, rows)], r1n, near),
        "to_far": (xb.at[pl.ds(pair + rows, rows)], r1f, far),
        "pg": (mv.at[piece(give0 + theirs0, sub)], lpg, near),
        "pk": (mv.at[piece(keep0 + theirs0, sub)], lpk, near),
        "px": (lpg, lpx, across),
        "pm": (lm2.at[piece(mine0, sub)], lm2.at[piece(mine0, sub)], near),
    }

    def copy(name):
        return remote(NUMBER[name], *routes[name])

    def go(*names):
        for name in names:
            copy(name).start()

    def arrived(*names):
        for name in names:
            copy(name).wait_recv()

    def sent(*names):
        for name in names:
            copy(name).wait_send()

    def link(name, i):
        here = piece(i * chunk, chunk)
        give = piece(give0 + i * chunk, chunk)
        src, dst, there = {
            "w1": (w_hbm.at[0, give], lw1.at[here], across),
            "w2": (lw1.at[here], lw2.at[here], near),
            "w3": (lw2.at[here], lw3.at[here], across),
            "m1": (mv.at[give], lm1.at[here], across),
            "m2": (lm1.at[here], lm2.at[here], near),
            "m3": (mv.at[piece(keep0 + i * chunk, chunk)], lm3.at[here], across),
            "g": (g_give.at[here], g_got.at[here], across),
        }[name]
        return remote(CHAINS[name] + i, src, dst, there)

    def load(k, src, dst):
        return pltpu.make_async_copy(src, dst, local.at[k])

    loads = [
        load(0, x_hbm.at[0], x0.at[pl.ds(0, rows)]),
        load(1, w_hbm.at[0], wv),
        load(2, og_hbm, og),
        load(3, x_hbm.at[1], xa.at[pl.ds(0, rows)]),
        load(4, m_hbm.at[0], mv),
    ]

    def each(count, body):
        @pl.loop(0, count)
        def _(i):
            body(i)

    loads[0].start()
    go("x0f0", "x0n0", "x0f1", "x0n1", "x0c0")
    each(CHUNKS, lambda i: link("w1", i).start())
    for load_now in loads[1:]:
        load_now.start()
    for k in "01":
        arrived("x0f" + k)
        go("x0fn" + k)
        arrived("x0n" + k)
        go("x0nf" + k)
    go("x1n0", "x1n1", "x1f", "x1c")
    loads[1].wait()

    def pair_chunk(own, landed, first, second, i):
        link(first, i).wait_recv()
        here = piece(i * chunk, chunk)
        mine = own[piece(keep0 + i * chunk, chunk), :].astype(f32)
        landed[here, :] = ((mine + landed[here, :].astype(f32)) * 0.5).astype(bf16)
        link(second, i).start()

    def mean(out, left, right):
        out[...] = ((left[...].astype(f32) + right[...].astype(f32)) * 0.5).astype(bf16)

    def w_pairs(first, last):
        each(last - first, lambda i: pair_chunk(wv, lw1, "w1", "w2", i + first))

    def m_pairs(first, last):
        each(last - first, lambda i: pair_chunk(mv, lm1, "m1", "m2", i + first))

    loads[0].wait()
    loads[2].wait()
    arrived("x0c0", "x0fn0", "x0fn1", "x0nf0", "x0nf1")
    go("x0c1")
    arrived("x0c1")

    depth = d // 8

    def product(lhs, rhs, starts, size):
        for first in starts:
            q_own[pl.ds(first, size), :] = jnp.zeros((size, cols), f32)

        def add(k):
            here = piece(k * depth, depth)
            left = jnp.concatenate([lhs[pl.ds(first, size), here] for first in starts], axis=0)
            more = dot(left, rhs[here, :], 1, 0)
            for at, first in enumerate(starts):
                q_own[pl.ds(first, size), :] += more[at * size : (at + 1) * size]

        each(d // depth, add)

    def slopes(out, step, pre):
        for j, block in enumerate((t, t_far, t_core, (t_core + 2) % 4)):
            up = og[step, piece(block * rows, rows), :].astype(f32)
            here = pl.ds(j * rows, rows)
            out[here, :] = (up * silu_slope(pre(here))).astype(bf16)

    product(x0, wv, (0,), 4 * rows)
    slopes(s0, 0, lambda here: q_own[here, :])
    loads[4].wait()

    def moment_tile(start):
        here = piece(start, chunk)
        grad = dot(x0[:, here], s0[...], 0, 0)
        moment = (mom_decay * mv[here, :].astype(f32) + grad).astype(bf16)
        mv[here, :] = moment
        stepped[here, :] = (wv[here, :].astype(f32) - learn_rate * moment.astype(f32)).astype(bf16)

    def moment_chunk(i):
        moment_tile(give0 + i * chunk)
        link("m1", i).start()

    each(direct, moment_chunk)
    each(CHUNKS - direct, lambda i: moment_tile(give0 + (i + direct) * chunk))
    go("pg")
    each(CHUNKS, lambda i: moment_tile(keep0 + i * chunk))
    go("st")

    sent("x0c1")
    arrived("x1n0")
    go("x1nf0")

    def part0(first):
        def one(k):
            here = piece(k * chunk, chunk)
            x0[pl.ds(first, pair), here] = dot(s0[pl.ds(first, pair), :], wv[here, :], 1, 1).astype(bf16)

        each(d // chunk, one)

    part0(pair)
    go("p0c")
    part0(0)

    arrived("x1n1")
    sent("x0fn0", "x0fn1", "x0nf0", "x0nf1")
    go("x1nf1")
    arrived("x1f")
    go("xbc")

    product(xb, stepped, (0,), pair)
    arrived("xbc")
    product(xb, stepped, (pair,), pair)
    q_give[...] = q_own[...].astype(bf16)
    go("q")
    w_pairs(0, 1)
    m_pairs(0, 1)
    w_pairs(1, 2)
    arrived("pg")
    mean(lpg, lpg, mv.at[piece(give0 + mine0, sub)])
    go("px")
    loads[3].wait()
    arrived("x1c")
    product(xa, stepped, (0, pair), rows)
    arrived("x1nf0", "x1nf1")
    go("x1c1")
    arrived("p0c")
    lp0[pl.ds(rows, rows), :] = (
        x0[pl.ds(rows, rows), :].astype(f32) + lp0[pl.ds(rows, rows), :].astype(f32)
    ).astype(bf16)
    arrived("x1c1")
    product(xa, stepped, (rows, pair + rows), rows)
    arrived("q")
    sent("p0c")
    slopes(s1, 1, lambda here: (q_own[here, :] + q_got[here, :].astype(f32)) * 0.5)
    go("s1n", "s1c", "pk")

    def chunk_of(ref, i):
        return ref.at[piece(i * chunk, chunk)]

    def step_weights(i):
        w_mean = chunk_of(lw2, i)
        w_mean[...] = (
            w_mean[...].astype(f32) - learn_rate * chunk_of(lm2, i)[...].astype(f32)
        ).astype(bf16)
        link("w3", i).start()

    def direct_means(i):
        link("w2", i).wait_recv()
        mean(chunk_of(lw2, i), chunk_of(lw2, i), chunk_of(lw1, i))
        link("m2", i).wait_recv()
        mean(chunk_of(lm2, i), chunk_of(lm2, i), chunk_of(lm1, i))
        step_weights(i)

    def gradient(start):
        return dot(xa[:, piece(start, chunk)], s1[...], 0, 0) * 0.5

    def gradient_chunk(i):
        g_give[piece(i * chunk, chunk), :] = gradient(give0 + i * chunk).astype(bf16)
        link("g", i).start()

    direct_means(0)
    each(CHUNKS, gradient_chunk)
    w_pairs(2, 3)
    m_pairs(1, 2)
    w_pairs(3, 4)
    m_pairs(2, direct)
    w_pairs(4, CHUNKS)
    arrived("s1n")
    go("s1bc")
    arrived("s1c", "s1bc", "st")

    sent("x1nf0", "x1nf1", "xbc")

    def part1(k):
        here = piece(k * chunk, chunk)
        mine = jnp.concatenate([s1[pl.ds(0, pair), :], s1b[pl.ds(0, pair), :]], axis=0)
        theirs = jnp.concatenate([s1o[...], s1bo[...]], axis=0)
        both = dot(mine, stepped[here, :], 1, 1) + dot(theirs, stepped_o[here, :], 1, 1)
        xb[:, here] = (both * 0.5).astype(bf16)

    each(d // chunk, part1)
    go("a1f", "to_far")

    each(direct - 1, lambda i: direct_means(i + 1))
    arrived("pk", "px")
    mean(lpk, lpk, mv.at[piece(keep0 + mine0, sub)])
    mean(lm2.at[piece(mine0, sub)], lpk, lpx)
    go("pm", "a0f")
    sent("pg", "pk")

    def finish_kept(i):
        link("g", i).wait_recv()
        here = piece(keep0 + i * chunk, chunk)
        grad = gradient(keep0 + i * chunk) + chunk_of(g_got, i)[...].astype(f32)
        moment = (mom_decay * chunk_of(lm2, i)[...].astype(f32) + grad).astype(bf16)
        mv[here, :] = moment
        link("m3", i).start()
        wv[here, :] = (
            chunk_of(lw2, i)[...].astype(f32) - learn_rate * moment.astype(f32)
        ).astype(bf16)

    arrived("a1f")
    here = pl.ds(pair, rows)
    xb[here, :] = (xb[here, :].astype(f32) + t1f[...].astype(f32)).astype(bf16)
    go("a0n", "to_near")
    each(direct, finish_kept)

    arrived("pm")

    def later_weights(i):
        link("w2", i).wait_recv()
        mean(chunk_of(lw2, i), chunk_of(lw2, i), chunk_of(lw1, i))
        step_weights(i)

    each(CHUNKS - direct, lambda i: later_weights(i + direct))
    each(CHUNKS - direct, lambda i: finish_kept(i + direct))
    arrived("a0f")
    go("a0fn")
    each(direct, lambda i: link("m1", i).wait_send())

    def finish_given(i):
        link("w3", i).wait_recv()
        link("m3", i).wait_recv()
        here = piece(give0 + i * chunk, chunk)
        moment = chunk_of(lm3, i)[...]
        mv[here, :] = moment
        wv[here, :] = (
            chunk_of(lw3, i)[...].astype(f32) - learn_rate * moment.astype(f32)
        ).astype(bf16)

    each(direct, finish_given)
    arrived("a0n")
    go("a0nf")

    def drain(i):
        for name in ("w1", "w2", "w3", "g"):
            link(name, i).wait_send()

    late = ("to_near", "to_far", "a0fn", "a0nf")
    each(CHUNKS, drain)
    each(direct, lambda i: link("m2", i).wait_send())
    sent(*[name for name in TRANSFERS if name not in AWAITED + late])
    arrived("to_near", "to_far")
    x_first = xb[pl.ds(0, rows), :].astype(f32)
    grad_in[1, :, :] = (x_first + r1n[...].astype(f32) + r1f[...].astype(f32)).astype(bf16)
    last = CHUNKS - 1
    each(last - direct, lambda i: finish_given(i + direct))
    each(last, lambda i: link("m3", i).wait_send())
    arrived("a0fn", "a0nf")
    for k, back in enumerate((r0n, r0f)):
        rows_of = pl.ds(k * cut, cut)
        grad_in[0, rows_of, :] = (
            x0[rows_of, :].astype(f32) + lp0[rows_of, :].astype(f32) + back[...].astype(f32)
        ).astype(bf16)
    sent(*late)
    finish_given(last)
    link("m3", last).wait_send()


def write_out(w_in, m_in, g_in, w_out, m_out, g_out, done):
    parts = 4
    size = w_in.shape[1] // parts
    pieces = [(g_in, g_out)]
    for k in range(parts):
        here = pl.ds(k * size, size)
        pieces += [(w_in.at[0, here], w_out.at[0, here]), (m_in.at[0, here], m_out.at[0, here])]
    copies = [
        pltpu.make_async_copy(src, dst, done.at[k]) for k, (src, dst) in enumerate(pieces)
    ]
    for c in copies:
        c.start()
    for c in copies:
        c.wait()


def local(weight, momentum, inputs, out_grads):
    d, cols = weight.shape[1:]
    rows = inputs.shape[1]
    n, pair, cut, half = 4 * rows, 2 * rows, rows // 2, d // 2
    full = (d, cols)
    vmem = (
        [(full, bf16)] * 2
        + [((n, d), bf16)] * 3
        + [((half, cols), bf16)] * 6
        + [((cut, d), bf16)] * 2
        + [((pair, d), bf16)]
        + [((rows, d), bf16)] * 2
        + [((n, cols), f32)]
        + [((n, cols), bf16)]
        + [((2, n, cols), bf16)]
        + [((n, cols), bf16)] * 2
        + [((pair, cols), bf16)] * 2
        + [((half, cols), bf16)] * 2
        + [((half // 4, cols), bf16)] * 3
    )
    results = pl.pallas_call(
        kernel,
        out_shape=(
            pltpu.VMEM(weight.shape, bf16),
            pltpu.VMEM(momentum.shape, bf16),
            pltpu.VMEM(inputs.shape, bf16),
        ),
        in_specs=[pl.BlockSpec(memory_space=pl.ANY)] * 4,
        out_specs=[pl.BlockSpec(memory_space=pltpu.VMEM)] * 3,
        scratch_shapes=[pltpu.VMEM(shape, kind) for shape, kind in vmem]
        + [
            pltpu.SemaphoreType.DMA((COPIES,)),
            pltpu.SemaphoreType.DMA((COPIES,)),
            pltpu.SemaphoreType.DMA((5,)),
        ],
        compiler_params=pltpu.CompilerParams(
            collective_id=0, has_side_effects=True, vmem_limit_bytes=53 << 20
        ),
    )(weight, momentum, inputs, out_grads)
    return pl.pallas_call(
        write_out,
        out_shape=[jax.ShapeDtypeStruct(a.shape, bf16) for a in (weight, momentum, inputs)],
        in_specs=[pl.BlockSpec(memory_space=pltpu.VMEM)] * 3,
        out_specs=[pl.BlockSpec(memory_space=pl.ANY)] * 3,
        scratch_shapes=[pltpu.SemaphoreType.DMA((9,))],
        compiler_params=pltpu.CompilerParams(vmem_limit_bytes=1 << 20),
    )(*results)


def solution(mesh):
    return jax.shard_map(
        local,
        mesh=mesh,
        in_specs=(
            P("replica", None, "tensor"),
            P("replica", None, "tensor"),
            P(None, ("replica", "tensor"), None),
            P(None, "replica", "tensor"),
        ),
        out_specs=(
            P("replica", None, "tensor"),
            P("replica", None, "tensor"),
            P(None, ("replica", "tensor"), None),
        ),
        check_vma=False,
    )
```
